128 devices in a mesh: wave: 32 (over x, y, core), lev: 4 (over z).
Axes of the slice: x: 4, y: 4, z: 4, core: 2. Of those that a mesh axis runs over, the one named last changes fastest.
Arguments:
- coefficients: bfloat16 [640, 640, 512], P('wave', 'lev'), may hold values from -6 to 6
- factors: bfloat16 [5, 2, 640, 20, 640], P(None, None, 'wave', None, 'lev'), may hold values from -1 to 1
- wave_ids: int32 [640], replicated, may hold values from 0 to 639, each once
Outputs:
- grid: bfloat16 [640, 256, 2560], P(('wave', 'lev'))
The draws below stay inside these ranges and needn't reach their ends.
Inputs may be any that keep to these rules, and one draw needn't show every extreme that they name: `wave_ids`: each wavenumber 0 .. 639 appears exactly once.
All inputs are finite; a program needn't handle non-finite values.
Results may differ from the reference program's by a relative error of at most 0.0079.
Values may be sent and summed in bfloat16 or wider, within the bound.
No kernel may reach another device: no remote copies, remote signals or barrier semaphores. Data moves between devices by JAX's collectives and lax.ppermute only.
A program may use at most 64 MiB of HBM per device.

```python
import math
import jax
import jax.numpy as jnp
from jax import lax

NDEG = 640
WAVES = 640
NLON = 2560
FIELDS = 8
LEVELS = 32
SECTIONS = 5
N_WAVE = 32
N_LEV = 4


def block_scale(rng, extent, shards, least, largest):
    gain = 1.0
    for position, shards_of in shards:
        draws = jax.random.uniform(jax.random.fold_in(jax.random.fold_in(rng, 6), position), (shards_of,), jnp.float32, least / len(shards), largest / len(shards))
        gain = gain * jnp.repeat(jnp.exp(draws), extent[position] // shards_of).reshape((-1,) + (1,) * (len(extent) - 1 - position))
    return gain


def noise(own_key, dims, scale, reach, cuts=(), held_as=jnp.bfloat16):
    array = jax.random.normal(own_key, dims, jnp.float32) * scale
    if len(cuts) > 0:
        array = block_scale(own_key, dims, cuts, -0.22, 0.18) * array
    return jnp.clip(array, min=-reach, max=reach).astype(held_as)


def setup_inputs(seed: int = 0) -> dict:
    arg_keys = jax.random.split(jax.random.key(seed), 4)
    return {
        "coefficients": noise(arg_keys[0], (NDEG, WAVES, 2 * FIELDS * LEVELS), 1.0, 6.0, ((0, 32), (1, 4))),
        "factors": noise(arg_keys[1], (SECTIONS, 2, NDEG, NDEG // N_WAVE, WAVES), (2 * NDEG // N_WAVE) ** -0.5, 1.0, ((2, 32), (4, 4))),
        "wave_ids": jax.random.permutation(arg_keys[2], WAVES).astype(jnp.int32),
    }


def reference(coefficients, factors, wave_ids):
    deg_block = NDEG // N_WAVE
    wave_block = WAVES // N_LEV
    channels = 2 * FIELDS * LEVELS
    degree = jnp.arange(NDEG, dtype=jnp.int32)

    def synthesize(block_index):
        offset = (block_index * wave_block).astype(jnp.int32)
        coef_block = lax.dynamic_slice_in_dim(coefficients, offset, wave_block, 1)
        own_ids = lax.dynamic_slice_in_dim(wave_ids, offset, wave_block, 0)
        live_mask = (degree[:, None] >= own_ids[None, :])[:, :, None]
        current = jnp.where(live_mask, coef_block, jnp.zeros((), coefficients.dtype))
        for section in range(SECTIONS):
            stride = 1 << section
            section_factors = lax.dynamic_slice_in_dim(factors[section], offset, wave_block, 3).astype(jnp.float32)
            self_factor = section_factors[0].reshape(N_WAVE, deg_block, deg_block, wave_block)
            partner_factor = section_factors[1].reshape(N_WAVE, deg_block, deg_block, wave_block)
            blocks_now = current.astype(jnp.float32).reshape(N_WAVE, deg_block, wave_block, channels)
            partner = blocks_now.reshape(N_WAVE // (2 * stride), 2, stride, deg_block, wave_block, channels)[:, ::-1]
            partner = partner.reshape(blocks_now.shape)
            combined = jnp.einsum('woim,wimc->womc', self_factor, blocks_now)
            combined = combined + jnp.einsum('woim,wimc->womc', partner_factor, partner)
            current = combined.reshape(NDEG, wave_block, channels).astype(jnp.bfloat16)
        return current
    blocks = lax.map(synthesize, jnp.arange(N_LEV, dtype=jnp.int32))
    lat_rows = jnp.transpose(blocks, (1, 0, 2, 3)).reshape(NDEG, WAVES, 2, FIELDS * LEVELS)
    longitude = jnp.arange(NLON, dtype=jnp.int32)
    phases = wave_ids[:, None] * longitude[None, :] % NLON
    angles = phases.astype(jnp.float32) * (2.0 * math.pi / NLON)
    weight = jnp.where(wave_ids == 0, 1.0, 2.0).astype(jnp.float32) / math.sqrt(2.0 * WAVES)
    cosine_part = weight[:, None] * jnp.cos(angles)
    sine_part = -weight[:, None] * jnp.sin(angles)
    fourier_table = jnp.stack([cosine_part, sine_part], axis=1).astype(jnp.bfloat16).astype(jnp.float32)
    lat_block = math.gcd(NDEG, 64)

    def fourier(block_index):
        offset = (block_index * lat_block).astype(jnp.int32)
        piece = lax.dynamic_slice_in_dim(lat_rows, offset, lat_block, 0).astype(jnp.float32)
        return jnp.einsum('rmpc,mpj->rcj', piece, fourier_table).astype(jnp.bfloat16)
    grid = lax.map(fourier, jnp.arange(NDEG // lat_block, dtype=jnp.int32))
    return grid.reshape(NDEG, FIELDS * LEVELS, NLON)
```

```python
import math

import jax
import jax.numpy as jnp
import numpy as np
from jax import lax
from jax.experimental import pallas as pl
from jax.experimental.pallas import tpu as pltpu
from jax.sharding import PartitionSpec as P

NLON = 2560
SECTIONS = 5
BLOCKS = 32
BANDS = 4
DEG = 20
OWN = 5
CH = 512
HALF = 256
ROWS = DEG * OWN
PADR = 112
SLOT = 56


def select_matrices():
    q = lax.broadcasted_iota(jnp.int32, (SECTIONS, 2, 256, 256), 2)
    lane = lax.broadcasted_iota(jnp.int32, (SECTIONS, 2, 256, 256), 3)
    s = lax.broadcasted_iota(jnp.int32, (SECTIONS, 2, 256, 256), 0)
    v = lax.broadcasted_iota(jnp.int32, (SECTIONS, 2, 256, 256), 1)
    part = (lane // 128) ^ v
    inner = lane % 128
    hit = (q == s * 40 + (inner % DEG) * 2 + part) & (inner < ROWS)
    return hit.astype(jnp.bfloat16)


def diagonal_mask():
    row = lax.broadcasted_iota(jnp.int32, (PADR, 256), 0)
    inner = lax.broadcasted_iota(jnp.int32, (PADR, 256), 1) % 128
    hit = (row // DEG == inner // DEG) & (row < ROWS) & (inner < ROWS)
    return hit.astype(jnp.float32)


def send_order():
    row = lax.broadcasted_iota(jnp.int32, (BANDS * SLOT, 256), 0)
    col = lax.broadcasted_iota(jnp.int32, (BANDS * SLOT, 256), 1)
    band, inner = row // SLOT, row % SLOT
    part, kr = inner // 25, inner % 25
    want = part * 128 + (kr // 5) * DEG + 5 * band + kr % 5
    return ((col == want) & (inner < 50)).astype(jnp.bfloat16)


def receive_order():
    row = lax.broadcasted_iota(jnp.int32, (400, 8 * SLOT), 0)
    col = lax.broadcasted_iota(jnp.int32, (400, 8 * SLOT), 1)
    part, lat = row // 200, (row // 40) % 5
    src, k = (row % 40) // 5, row % 5
    return (col == src * SLOT + part * 25 + k * 5 + lat).astype(jnp.bfloat16)


def butterfly_kernel(rx_ref, e_ref, mask_ref, first_ref, order_ref, out_ref, xa, xb, fc):
    zeros_x = jnp.zeros((32, CH), jnp.bfloat16)
    zeros_f = jnp.zeros((16, 256), jnp.bfloat16)

    def load(b, carry):
        xa[b, pl.ds(96, 32), :] = zeros_x
        xb[b, pl.ds(96, 32), :] = zeros_x
        fc[b, pl.ds(96, 16), :] = zeros_f
        xa[b, pl.ds(0, ROWS), :] = rx_ref[b, :, :CH]
        fc[b, pl.ds(0, ROWS), :] = rx_ref[b, :, CH:]
        return carry

    lax.fori_loop(0, BLOCKS, load, 0)
    lane_high = lax.broadcasted_iota(jnp.int32, (8, 256), 1) // 128
    bufs = (xa, xb)
    for s in range(SECTIONS):
        src, dst = bufs[s % 2], bufs[(s + 1) % 2]

        def pair(j, carry, s=s, src=src, dst=dst):
            low = (j >> s) * (2 << s) + (j & ((1 << s) - 1))
            high = low + (1 << s)
            mask = mask_ref[...]
            if s == 0:
                start = DEG * (low + lane_high * (1 << s))
                live = (start >= first_ref[...]).astype(jnp.float32)
                mask = mask * live[0:1, :]
            f_low = jnp.dot(fc[low], e_ref[s, 0], preferred_element_type=jnp.float32) * mask
            f_high = jnp.dot(fc[high], e_ref[s, 1], preferred_element_type=jnp.float32) * mask
            left = jnp.concatenate([f_low.astype(jnp.bfloat16), f_high.astype(jnp.bfloat16)], axis=0)
            right = jnp.concatenate([src[low], src[high]], axis=0)
            y = jnp.dot(left, right, preferred_element_type=jnp.float32).astype(jnp.bfloat16)
            dst[low, pl.ds(0, PADR), :] = y[:PADR]
            dst[high, pl.ds(0, PADR), :] = y[PADR:]
            return carry

        lax.fori_loop(0, BLOCKS // 2, pair, 0, unroll=2)
    last = bufs[SECTIONS % 2]

    def emit(b, carry):
        right = jnp.concatenate([last[b, :, :HALF], last[b, :, HALF:]], axis=0)
        y = jnp.dot(order_ref[...], right, preferred_element_type=jnp.float32)
        for band in range(BANDS):
            out_ref[BANDS * b + band] = y[band * SLOT:(band + 1) * SLOT].astype(jnp.bfloat16)
        return carry

    lax.fori_loop(0, BLOCKS, emit, 0, unroll=2)


def butterfly(rx, first):
    return pl.pallas_call(
        butterfly_kernel,
        out_shape=jax.ShapeDtypeStruct((BLOCKS * BANDS, SLOT, HALF), jnp.bfloat16),
        scratch_shapes=[
            pltpu.VMEM((BLOCKS, 128, CH), jnp.bfloat16),
            pltpu.VMEM((BLOCKS, 128, CH), jnp.bfloat16),
            pltpu.VMEM((BLOCKS, PADR, 256), jnp.bfloat16),
        ],
        compiler_params=pltpu.CompilerParams(vmem_limit_bytes=60 << 20),
        name="butterfly",
    )(rx, select_matrices(), diagonal_mask(), first, send_order())


def fourier_kernel(u_ref, order_ref, table_ref, out_ref, v):
    @pl.when(pl.program_id(0) == 0)
    def _():
        for g in range(16):
            piece = u_ref[pl.ds(8 * g, 8)].reshape(8 * SLOT, HALF)
            y = jnp.dot(order_ref[...], piece, preferred_element_type=jnp.float32)
            for p in range(2):
                for r in range(5):
                    at = p * 200 + r * 40
                    v[r, pl.ds(p * 640 + 40 * g, 40), :] = y[at:at + 40].astype(jnp.bfloat16)

    for r in range(5):
        y = lax.dot_general(v[r], table_ref[...], (((0,), (0,)), ((), ())), preferred_element_type=jnp.float32)
        out_ref[r] = y.astype(jnp.bfloat16)


def fourier(u, table):
    tile = 256
    return pl.pallas_call(
        fourier_kernel,
        out_shape=jax.ShapeDtypeStruct((5, HALF, NLON), jnp.bfloat16),
        grid=(NLON // tile,),
        in_specs=[
            pl.BlockSpec((BLOCKS * BANDS, SLOT, HALF), lambda j: (0, 0, 0)),
            pl.BlockSpec((400, 8 * SLOT), lambda j: (0, 0)),
            pl.BlockSpec((1280, tile), lambda j: (0, j)),
        ],
        out_specs=pl.BlockSpec((5, HALF, tile), lambda j: (0, 0, j)),
        scratch_shapes=[pltpu.VMEM((5, 1280, HALF), jnp.bfloat16)],
        compiler_params=pltpu.CompilerParams(vmem_limit_bytes=60 << 20),
        name="fourier",
    )(u, receive_order(), table)


def fourier_table(ids):
    longitude = jnp.arange(NLON, dtype=jnp.int32)
    phases = ids[:, None] * longitude[None, :] % NLON
    angles = phases.astype(jnp.float32) * (2.0 * math.pi / NLON)
    weight = jnp.where(ids == 0, 1.0, 2.0).astype(jnp.float32) / math.sqrt(2.0 * ids.shape[0])
    cosine_part = weight[:, None] * jnp.cos(angles)
    sine_part = -weight[:, None] * jnp.sin(angles)
    return jnp.concatenate([cosine_part, sine_part], axis=0).astype(jnp.bfloat16)


def body(coefficients, factors, wave_ids):
    wave_pos = lax.axis_index("wave")
    lev_pos = lax.axis_index("lev")
    flat = factors.transpose(2, 4, 0, 3, 1).reshape(DEG, OWN * BLOCKS, 200)
    flat = jnp.pad(flat, ((0, 0), (0, 0), (0, 56)))
    joined = jnp.concatenate([coefficients, flat], axis=2)
    send = joined.reshape(DEG, BLOCKS, OWN, 768).transpose(1, 2, 0, 3).reshape(BLOCKS, ROWS, 768)
    rx = lax.all_to_all(send, "wave", 0, 0, tiled=True)
    own_ids = lax.dynamic_slice_in_dim(wave_ids, lev_pos * (OWN * BLOCKS) + wave_pos * OWN, OWN, 0)
    first = (own_ids[:, None] - jnp.arange(DEG, dtype=jnp.int32)[None, :]).reshape(ROWS)
    first = jnp.pad(first, (0, 28))
    first = jnp.broadcast_to(jnp.concatenate([first, first])[None, :], (8, 256))
    rows = butterfly(rx, first)
    u = lax.all_to_all(rows, ("wave", "lev"), 0, 0, tiled=True)
    ids = wave_ids.reshape(BANDS, BLOCKS, OWN).transpose(1, 0, 2).reshape(-1)
    return fourier(u, fourier_table(ids))


def solution(mesh):
    in_specs = (P("wave", "lev", None), P(None, None, "wave", None, "lev"), P())
    out_specs = P(("wave", "lev"), None, None)
    return jax.shard_map(body, mesh=mesh, in_specs=in_specs, out_specs=out_specs, check_vma=False)
```

```python
import math

import jax
import jax.numpy as jnp
import numpy as np
from jax import lax
from jax.experimental import pallas as pl
from jax.experimental.pallas import tpu as pltpu
from jax.sharding import PartitionSpec as P

NLON = 2560
SECTIONS = 5
BLOCKS = 32
BANDS = 4
DEG = 20
OWN = 5
CH = 512
HALF = 256
ROWS = DEG * OWN
PADR = 112
SLOT = 56
PAIR = 2 * PADR


def select_matrices():
    shape = (SECTIONS, 2, 256, PAIR)
    s, v, q, lane = (lax.broadcasted_iota(jnp.int32, shape, d) for d in range(4))
    part = (lane // PADR) ^ v
    inner = lane % PADR
    hit = (q == s * 40 + (inner % DEG) * 2 + part) & (inner < ROWS)
    return hit.astype(jnp.bfloat16)


def diagonal_mask():
    row = lax.broadcasted_iota(jnp.int32, (PADR, PAIR), 0)
    inner = lax.broadcasted_iota(jnp.int32, (PADR, PAIR), 1) % PADR
    hit = (row // DEG == inner // DEG) & (row < ROWS) & (inner < ROWS)
    return hit.astype(jnp.float32)


def send_order():
    row = lax.broadcasted_iota(jnp.int32, (BANDS * SLOT, PAIR), 0)
    col = lax.broadcasted_iota(jnp.int32, (BANDS * SLOT, PAIR), 1)
    band, inner = row // SLOT, row % SLOT
    part, kr = inner // 25, inner % 25
    want = part * PADR + (kr // 5) * DEG + 5 * band + kr % 5
    return ((col == want) & (inner < 50)).astype(jnp.bfloat16)


def fill_pack_order(order):
    shape = (4 * 104, DEG * 32)
    row = lax.broadcasted_iota(jnp.int32, shape, 0)
    col = lax.broadcasted_iota(jnp.int32, shape, 1)
    owner = (row >= 104).astype(jnp.int32) + (row >= 208).astype(jnp.int32) + (row >= 312).astype(jnp.int32)
    inner = row - 104 * owner
    k = sum((inner >= DEG * i).astype(jnp.int32) for i in range(1, OWN))
    base = (inner - DEG * k) * 32 + OWN * owner + k
    ahead = jnp.where(inner < ROWS, col - base, -1)
    for v in range(4):
        order[v] = (ahead == 4 * v).astype(jnp.float32).astype(jnp.bfloat16)


def pack_rows(src, order_ref, out_ref):
    for group in range(BLOCKS // 4):
        start = 4 * OWN * group
        at = start // 16 * 16
        window = src[:, at:at + 32, :]
        window = window.reshape(DEG * 32, window.shape[2])
        y = jnp.dot(order_ref[(start - at) // 4], window, preferred_element_type=jnp.float32)
        for d in range(4):
            out_ref[4 * group + d] = y[104 * d:104 * d + ROWS].astype(jnp.bfloat16)


def pack_factors_kernel(f_ref, eye_ref, out_ref, turned, order):
    fill_pack_order(order)
    for o in range(DEG):
        left = jnp.concatenate([f_ref[s, o].reshape(2 * DEG, OWN * BLOCKS) for s in range(SECTIONS)], axis=0)
        y = lax.dot_general(left, eye_ref[...], (((0,), (0,)), ((), ())), preferred_element_type=jnp.float32)
        turned[o] = y.astype(jnp.bfloat16)
    pack_rows(turned, order, out_ref)


def pack_factors(factors):
    return pl.pallas_call(
        pack_factors_kernel,
        out_shape=jax.ShapeDtypeStruct((BLOCKS, ROWS, 256), jnp.bfloat16),
        scratch_shapes=[pltpu.VMEM((DEG, OWN * BLOCKS, 256), jnp.bfloat16), pltpu.VMEM((4, 416, 640), jnp.bfloat16)],
        compiler_params=pltpu.CompilerParams(vmem_limit_bytes=60 << 20),
        name="pack_factors",
    )(factors.transpose(0, 2, 3, 1, 4), jnp.asarray(np.eye(200, 256), jnp.bfloat16))


def pack_coefficients_kernel(x_ref, out_ref, order):
    @pl.when(pl.program_id(0) == 0)
    def _():
        fill_pack_order(order)

    pack_rows(x_ref, order, out_ref)


def pack_coefficients(x):
    return pl.pallas_call(
        pack_coefficients_kernel,
        out_shape=jax.ShapeDtypeStruct((BLOCKS, ROWS, CH), jnp.bfloat16),
        grid=(2,),
        in_specs=[pl.BlockSpec((DEG, OWN * BLOCKS, HALF), lambda i: (0, 0, i))],
        out_specs=pl.BlockSpec((BLOCKS, ROWS, HALF), lambda i: (0, 0, i)),
        scratch_shapes=[pltpu.VMEM((4, 416, 640), jnp.bfloat16)],
        compiler_params=pltpu.CompilerParams(vmem_limit_bytes=60 << 20),
        name="pack_coefficients",
    )(x)


def receive_order():
    row = lax.broadcasted_iota(jnp.int32, (400, 8 * SLOT), 0)
    col = lax.broadcasted_iota(jnp.int32, (400, 8 * SLOT), 1)
    part, lat = row // 200, (row // 40) % 5
    src, k = (row % 40) // 5, row % 5
    return (col == src * SLOT + part * 25 + k * 5 + lat).astype(jnp.bfloat16)


def lower_block(s, group, j):
    if s < 3:
        return 8 * group + (j >> s) * (2 << s) + (j & ((1 << s) - 1))
    step = 16 if s == 3 else 8
    return 2 * group + j // 2 + step * (j % 2)


def section_kernel(rf_ref, e_ref, mask_ref, first_ref, near_ref, far_ref, fc):
    zeros_f = jnp.zeros((16, 256), jnp.bfloat16)

    def load(b, carry):
        fc[b, pl.ds(96, 16), :] = zeros_f
        fc[b, pl.ds(0, ROWS), :] = rf_ref[b]
        return carry

    lax.fori_loop(0, BLOCKS, load, 0)
    lane_high = lax.broadcasted_iota(jnp.int32, (8, PAIR), 1) // PADR
    mask = mask_ref[...]
    for s in range(SECTIONS):
        lows = [(g, j, lower_block(s, g, j)) for g in range(4) for j in range(4)]
        for v in range(2):
            left = jnp.concatenate([fc[low + (v << s)] for _, _, low in lows], axis=0)
            f = jnp.dot(left, e_ref[s, v], preferred_element_type=jnp.float32)
            for i, (g, j, low) in enumerate(lows):
                keep = mask
                if s == 0:
                    start = DEG * (low + lane_high)
                    live = (start >= first_ref[...]).astype(jnp.float32)
                    keep = mask * live[0:1, :]
                piece = (f[i * PADR:(i + 1) * PADR] * keep).astype(jnp.bfloat16)
                if s < 3:
                    near_ref[g, 4 * s + j, pl.ds(v * PADR, PADR), :] = piece
                else:
                    far_ref[g, 4 * (s - 3) + j, pl.ds(v * PADR, PADR), :] = piece


def section_factors(rf, first):
    return pl.pallas_call(
        section_kernel,
        out_shape=[
            jax.ShapeDtypeStruct((4, 12, PAIR, PAIR), jnp.bfloat16),
            jax.ShapeDtypeStruct((4, 8, PAIR, PAIR), jnp.bfloat16),
        ],
        scratch_shapes=[pltpu.VMEM((BLOCKS, PADR, 256), jnp.bfloat16)],
        compiler_params=pltpu.CompilerParams(vmem_limit_bytes=58 << 20),
        name="section_factors",
    )(rf, select_matrices(), diagonal_mask(), first)


def butterfly_kernel(rx_ref, near_ref, far_ref, order_ref, out_ref, xa, xb, xc, xd):
    step = pl.program_id(0)

    @pl.when(step == 0)
    def _():
        for b in range(8):
            xa[b, pl.ds(96, 16), :] = jnp.zeros((16, CH), jnp.bfloat16)

    @pl.when(step < 4)
    def _():
        for b in range(8):
            xa[b, pl.ds(0, ROWS), :] = rx_ref[b]
        src, dst = xa, xb
        for s in range(3):
            base = 8 * step if s == 2 else 0
            out = xc if s == 2 else dst
            for j in range(4):
                low = lower_block(s, 0, j)
                high = low + (1 << s)
                right = jnp.concatenate([src[low], src[high]], axis=0)
                y = jnp.dot(near_ref[0, 4 * s + j], right, preferred_element_type=jnp.float32).astype(jnp.bfloat16)
                out[base + low] = y[:PADR]
                out[base + high] = y[PADR:]
            src, dst = dst, src

    @pl.when(step >= 4)
    def _():
        first = 2 * (step - 4)
        for j in range(4):
            r, h = j // 2, j % 2
            low = first + r + 16 * h
            right = jnp.concatenate([xc[low], xc[low + 8]], axis=0)
            y = jnp.dot(far_ref[0, j], right, preferred_element_type=jnp.float32).astype(jnp.bfloat16)
            xd[r, 2 * h] = y[:PADR]
            xd[r, 2 * h + 1] = y[PADR:]
        for j in range(4):
            r, h = j // 2, j % 2
            right = jnp.concatenate([xd[r, h], xd[r, h + 2]], axis=0)
            y = jnp.dot(far_ref[0, 4 + j], right, preferred_element_type=jnp.float32).astype(jnp.bfloat16)
            for half in range(2):
                rows = y[half * PADR:(half + 1) * PADR]
                right = jnp.concatenate([rows[:, :HALF], rows[:, HALF:]], axis=0)
                z = jnp.dot(order_ref[...], right, preferred_element_type=jnp.float32)
                for band in range(BANDS):
                    out_ref[h + 2 * half, r, band] = z[band * SLOT:(band + 1) * SLOT].astype(jnp.bfloat16)


def butterfly(rx, near, far):
    early = lambda i: jnp.minimum(i, 3)
    late = lambda i: jnp.maximum(i - 4, 0)
    rows = pl.pallas_call(
        butterfly_kernel,
        out_shape=jax.ShapeDtypeStruct((4, 8, BANDS, SLOT, HALF), jnp.bfloat16),
        grid=(8,),
        in_specs=[
            pl.BlockSpec((8, ROWS, CH), lambda i: (early(i), 0, 0)),
            pl.BlockSpec((1, 12, PAIR, PAIR), lambda i: (early(i), 0, 0, 0)),
            pl.BlockSpec((1, 8, PAIR, PAIR), lambda i: (late(i), 0, 0, 0)),
            pl.BlockSpec((BANDS * SLOT, PAIR), lambda i: (0, 0)),
        ],
        out_specs=pl.BlockSpec((4, 2, BANDS, SLOT, HALF), lambda i: (0, late(i), 0, 0, 0)),
        scratch_shapes=[
            pltpu.VMEM((8, PADR, CH), jnp.bfloat16),
            pltpu.VMEM((8, PADR, CH), jnp.bfloat16),
            pltpu.VMEM((BLOCKS, PADR, CH), jnp.bfloat16),
            pltpu.VMEM((2, 4, PADR, CH), jnp.bfloat16),
        ],
        compiler_params=pltpu.CompilerParams(vmem_limit_bytes=56 << 20),
        name="butterfly",
    )(rx, near, far, send_order())
    return rows.reshape(BLOCKS * BANDS, SLOT, HALF)


def mirror_order():
    row = lax.broadcasted_iota(jnp.int32, (256, 256), 0)
    lane = lax.broadcasted_iota(jnp.int32, (256, 256), 1)
    return (row + lane == 256).astype(jnp.bfloat16)


def fourier_kernel(u_ref, order_ref, mirror_ref, table_ref, middle_ref, out_ref, v, vt, edge, buf, sem):
    step = pl.program_id(0)
    slot = step % 2
    tile = 256

    def copies(at, into):
        near = pltpu.make_async_copy(buf.at[into, 0], out_ref.at[:, :, pl.ds((4 - at) * tile, tile)], sem.at[into, 0])
        far = pltpu.make_async_copy(buf.at[into, 1], out_ref.at[:, :, pl.ds((5 + at) * tile, tile)], sem.at[into, 1])
        return near, far

    def sums(table):
        even = jnp.dot(vt[:, :640], table[:640], preferred_element_type=jnp.float32)
        odd = jnp.dot(vt[:, 640:], table[640:], preferred_element_type=jnp.float32)
        return even, odd

    @pl.when(step == 0)
    def _():
        for g in range(16):
            piece = u_ref[pl.ds(8 * g, 8)].reshape(8 * SLOT, HALF)
            y = jnp.dot(order_ref[...], piece, preferred_element_type=jnp.float32)
            for p in range(2):
                for r in range(5):
                    at = p * 200 + r * 40
                    v[r, pl.ds(p * 640 + 40 * g, 40), :] = y[at:at + 40].astype(jnp.bfloat16)
        for r in range(5):
            vt[pl.ds(r * HALF, HALF), :] = v[r].T
        even, odd = sums(middle_ref[...])
        edge[...] = even - odd

    @pl.when(step >= 2)
    def _():
        for copy in copies(step - 2, slot):
            copy.wait()

    even, odd = sums(table_ref[...])
    near = (even + odd).astype(jnp.bfloat16)
    far = (even - odd).astype(jnp.bfloat16)
    turned = jnp.dot(far, mirror_ref[...], preferred_element_type=jnp.float32)
    lane = lax.broadcasted_iota(jnp.int32, (5 * HALF, 128), 1)
    head = jnp.where(lane == 0, edge[...], turned[:, :128]).astype(jnp.bfloat16)
    tail = turned[:, 128:].astype(jnp.bfloat16)
    edge[...] = far[:, :128].astype(jnp.float32)
    for r in range(5):
        rows = slice(r * HALF, (r + 1) * HALF)
        buf[slot, 0, r] = near[rows]
        buf[slot, 1, r, :, pl.ds(0, 128)] = head[rows]
        buf[slot, 1, r, :, pl.ds(128, 128)] = tail[rows]
    for copy in copies(step, slot):
        copy.start()

    @pl.when(step == 4)
    def _():
        for copy in copies(3, 1) + copies(4, 0):
            copy.wait()


def fourier(u, table):
    return pl.pallas_call(
        fourier_kernel,
        out_shape=jax.ShapeDtypeStruct((5, HALF, NLON), jnp.bfloat16),
        grid=(5,),
        in_specs=[
            pl.BlockSpec((BLOCKS * BANDS, SLOT, HALF), lambda j: (0, 0, 0)),
            pl.BlockSpec((400, 8 * SLOT), lambda j: (0, 0)),
            pl.BlockSpec((256, 256), lambda j: (0, 0)),
            pl.BlockSpec((1280, 256), lambda j: (0, 4 - j)),
            pl.BlockSpec((1280, 128), lambda j: (0, 10)),
        ],
        out_specs=pl.BlockSpec(memory_space=pl.ANY),
        scratch_shapes=[
            pltpu.VMEM((5, 1280, HALF), jnp.bfloat16),
            pltpu.VMEM((5 * HALF, 1280), jnp.bfloat16),
            pltpu.VMEM((5 * HALF, 128), jnp.float32),
            pltpu.VMEM((2, 2, 5, HALF, 256), jnp.bfloat16),
            pltpu.SemaphoreType.DMA((2, 2)),
        ],
        compiler_params=pltpu.CompilerParams(vmem_limit_bytes=60 << 20),
        name="fourier",
    )(u, receive_order(), mirror_order(), table, table)


def fourier_table(ids):
    longitude = jnp.arange(NLON // 2 + 128, dtype=jnp.int32)
    phases = ids[:, None] * longitude[None, :] % NLON
    angles = phases.astype(jnp.float32) * (2.0 * math.pi / NLON)
    weight = jnp.where(ids == 0, 1.0, 2.0).astype(jnp.float32) / math.sqrt(2.0 * ids.shape[0])
    cosine_part = weight[:, None] * jnp.cos(angles)
    sine_part = -weight[:, None] * jnp.sin(angles)
    return jnp.concatenate([cosine_part, sine_part], axis=0).astype(jnp.bfloat16)


def body(coefficients, factors, wave_ids):
    wave_pos = lax.axis_index("wave")
    lev_pos = lax.axis_index("lev")
    rf = lax.all_to_all(pack_factors(factors), "wave", 0, 0, tiled=True)
    send_x, rf = lax.optimization_barrier((pack_coefficients(coefficients), rf))
    rx = lax.all_to_all(send_x, "wave", 0, 0, tiled=True)
    own_ids = lax.dynamic_slice_in_dim(wave_ids, lev_pos * (OWN * BLOCKS) + wave_pos * OWN, OWN, 0)
    first = (own_ids[:, None] - jnp.arange(DEG, dtype=jnp.int32)[None, :]).reshape(ROWS)
    first = jnp.pad(first, (0, PADR - ROWS))
    first = jnp.broadcast_to(jnp.concatenate([first, first])[None, :], (8, PAIR))
    near, far = section_factors(rf, first)
    rows = butterfly(rx, near, far)
    u = lax.all_to_all(rows, ("wave", "lev"), 0, 0, tiled=True)
    ids = wave_ids.reshape(BANDS, BLOCKS, OWN).transpose(1, 0, 2).reshape(-1)
    return fourier(u, fourier_table(ids))


def solution(mesh):
    in_specs = (P("wave", "lev", None), P(None, None, "wave", None, "lev"), P())
    out_specs = P(("wave", "lev"), None, None)
    return jax.shard_map(body, mesh=mesh, in_specs=in_specs, out_specs=out_specs, check_vma=False)
```

```python
import math

import jax
import jax.numpy as jnp
import numpy as np
from jax import lax
from jax.experimental import pallas as pl
from jax.experimental.pallas import tpu as pltpu
from jax.sharding import PartitionSpec as P

NLON = 2560
SECTIONS = 5
BLOCKS = 32
BANDS = 4
DEG = 20
OWN = 5
CH = 512
PART = 256
HALF = 128
ROWS = DEG * OWN
PADR = 112
SLOT = 56
PAIR = 2 * PADR


def select_matrices():
    shape = (SECTIONS, 2, 256, PAIR)
    s, v, q, lane = (lax.broadcasted_iota(jnp.int32, shape, d) for d in range(4))
    part = (lane // PADR) ^ v
    inner = lane % PADR
    hit = (q == s * 40 + (inner % DEG) * 2 + part) & (inner < ROWS)
    return hit.astype(jnp.bfloat16)


def diagonal_mask():
    row = lax.broadcasted_iota(jnp.int32, (PADR, PAIR), 0)
    inner = lax.broadcasted_iota(jnp.int32, (PADR, PAIR), 1) % PADR
    hit = (row // DEG == inner // DEG) & (row < ROWS) & (inner < ROWS)
    return hit.astype(jnp.float32)


def send_order():
    row = lax.broadcasted_iota(jnp.int32, (BANDS * SLOT, PAIR), 0)
    col = lax.broadcasted_iota(jnp.int32, (BANDS * SLOT, PAIR), 1)
    band, inner = row // SLOT, row % SLOT
    part, kr = inner // 25, inner % 25
    want = part * PADR + (kr // 5) * DEG + 5 * band + kr % 5
    return ((col == want) & (inner < 50)).astype(jnp.bfloat16)


def fill_pack_order(order):
    shape = (4 * 104, DEG * 32)
    row = lax.broadcasted_iota(jnp.int32, shape, 0)
    col = lax.broadcasted_iota(jnp.int32, shape, 1)
    owner = (row >= 104).astype(jnp.int32) + (row >= 208).astype(jnp.int32) + (row >= 312).astype(jnp.int32)
    inner = row - 104 * owner
    k = sum((inner >= DEG * i).astype(jnp.int32) for i in range(1, OWN))
    base = (inner - DEG * k) * 32 + OWN * owner + k
    ahead = jnp.where(inner < ROWS, col - base, -1)
    for v in range(4):
        order[v] = (ahead == 4 * v).astype(jnp.float32).astype(jnp.bfloat16)


def pack_rows(srcs, order, out_ref):
    for group in range(BLOCKS // 4):
        start = 4 * OWN * group
        at = start // 16 * 16
        window = jnp.concatenate([src[:, at:at + 32, :].reshape(DEG * 32, src.shape[2]) for src in srcs], axis=1)
        y = jnp.dot(order[(start - at) // 4], window, preferred_element_type=jnp.float32)
        for d in range(4):
            out_ref[4 * group + d] = y[104 * d:104 * d + ROWS].astype(jnp.bfloat16)


def pack_first_kernel(f_ref, eye_ref, x_ref, out_ref, turned, order, xs, sem):
    fetch = [
        pltpu.make_async_copy(x_ref.at[:, :, pl.ds(p * PART, HALF)], xs.at[:, :, pl.ds(p * HALF, HALF)], sem.at[p])
        for p in range(2)
    ]

    @pl.when(pl.program_id(0) == 0)
    def _():
        for copy in fetch:
            copy.start()
        fill_pack_order(order)
        for o in range(DEG):
            left = jnp.concatenate([f_ref[s, o].reshape(2 * DEG, OWN * BLOCKS) for s in range(SECTIONS)], axis=0)
            y = lax.dot_general(left, eye_ref[...], (((0,), (0,)), ((), ())), preferred_element_type=jnp.float32)
            turned[o] = y.astype(jnp.bfloat16)
        pack_rows([turned], order, out_ref)

    @pl.when(pl.program_id(0) == 1)
    def _():
        for copy in fetch:
            copy.wait()
        pack_rows([xs], order, out_ref)


def pack_first(factors, x):
    return pl.pallas_call(
        pack_first_kernel,
        out_shape=jax.ShapeDtypeStruct((BLOCKS, ROWS, 2 * PART), jnp.bfloat16),
        grid=(2,),
        in_specs=[
            pl.BlockSpec((SECTIONS, DEG, DEG, 2, OWN * BLOCKS), lambda i: (0, 0, 0, 0, 0)),
            pl.BlockSpec((200, 256), lambda i: (0, 0)),
            pl.BlockSpec(memory_space=pl.ANY),
        ],
        out_specs=pl.BlockSpec((BLOCKS, ROWS, PART), lambda i: (0, 0, i)),
        scratch_shapes=[
            pltpu.VMEM((DEG, OWN * BLOCKS, 256), jnp.bfloat16),
            pltpu.VMEM((4, 416, 640), jnp.bfloat16),
            pltpu.VMEM((DEG, OWN * BLOCKS, PART), jnp.bfloat16),
            pltpu.SemaphoreType.DMA((2,)),
        ],
        compiler_params=pltpu.CompilerParams(vmem_limit_bytes=60 << 20),
        name="pack_first",
    )(factors.transpose(0, 2, 3, 1, 4), jnp.asarray(np.eye(200, 256), jnp.bfloat16), x)


def pack_second_kernel(re_ref, im_ref, out_ref, order):
    fill_pack_order(order)
    pack_rows([re_ref, im_ref], order, out_ref)


def pack_second(x):
    return pl.pallas_call(
        pack_second_kernel,
        out_shape=jax.ShapeDtypeStruct((BLOCKS, ROWS, PART), jnp.bfloat16),
        grid=(1,),
        in_specs=[
            pl.BlockSpec((DEG, OWN * BLOCKS, HALF), lambda i: (0, 0, 1)),
            pl.BlockSpec((DEG, OWN * BLOCKS, HALF), lambda i: (0, 0, 3)),
        ],
        out_specs=pl.BlockSpec((BLOCKS, ROWS, PART), lambda i: (0, 0, 0)),
        scratch_shapes=[pltpu.VMEM((4, 416, 640), jnp.bfloat16)],
        compiler_params=pltpu.CompilerParams(vmem_limit_bytes=60 << 20),
        name="pack_second",
    )(x, x)


def receive_order():
    row = lax.broadcasted_iota(jnp.int32, (400, 8 * SLOT), 0)
    col = lax.broadcasted_iota(jnp.int32, (400, 8 * SLOT), 1)
    part, lat = row // 200, (row // 40) % 5
    src, k = (row % 40) // 5, row % 5
    return (col == src * SLOT + part * 25 + k * 5 + lat).astype(jnp.bfloat16)


def lower_block(s, group, j):
    if s < 3:
        return 8 * group + (j >> s) * (2 << s) + (j & ((1 << s) - 1))
    step = 16 if s == 3 else 8
    return 2 * group + j // 2 + step * (j % 2)


def section_kernel(rf_ref, e_ref, mask_ref, first_ref, near_ref, far_ref, fc):
    zeros_f = jnp.zeros((16, 256), jnp.bfloat16)

    def load(b, carry):
        fc[b, pl.ds(96, 16), :] = zeros_f
        fc[b, pl.ds(0, ROWS), :] = rf_ref[b]
        return carry

    lax.fori_loop(0, BLOCKS, load, 0)
    lane_high = lax.broadcasted_iota(jnp.int32, (8, PAIR), 1) // PADR
    mask = mask_ref[...]
    for s in range(SECTIONS):
        lows = [(g, j, lower_block(s, g, j)) for g in range(4) for j in range(4)]
        for v in range(2):
            left = jnp.concatenate([fc[low + (v << s)] for _, _, low in lows], axis=0)
            f = jnp.dot(left, e_ref[s, v], preferred_element_type=jnp.float32)
            for i, (g, j, low) in enumerate(lows):
                keep = mask
                if s == 0:
                    start = DEG * (low + lane_high)
                    live = (start >= first_ref[...]).astype(jnp.float32)
                    keep = mask * live[0:1, :]
                piece = (f[i * PADR:(i + 1) * PADR] * keep).astype(jnp.bfloat16)
                if s < 3:
                    near_ref[g, 4 * s + j, pl.ds(v * PADR, PADR), :] = piece
                else:
                    far_ref[g, 4 * (s - 3) + j, pl.ds(v * PADR, PADR), :] = piece


def section_factors(rf, first):
    return pl.pallas_call(
        section_kernel,
        out_shape=[
            jax.ShapeDtypeStruct((4, 12, PAIR, PAIR), jnp.bfloat16),
            jax.ShapeDtypeStruct((4, 8, PAIR, PAIR), jnp.bfloat16),
        ],
        grid=(1,),
        in_specs=[
            pl.BlockSpec((BLOCKS, ROWS, 256), lambda i: (0, 0, 0)),
            pl.BlockSpec((SECTIONS, 2, 256, PAIR), lambda i: (0, 0, 0, 0)),
            pl.BlockSpec((PADR, PAIR), lambda i: (0, 0)),
            pl.BlockSpec((8, PAIR), lambda i: (0, 0)),
        ],
        out_specs=[
            pl.BlockSpec((4, 12, PAIR, PAIR), lambda i: (0, 0, 0, 0)),
            pl.BlockSpec((4, 8, PAIR, PAIR), lambda i: (0, 0, 0, 0)),
        ],
        scratch_shapes=[pltpu.VMEM((BLOCKS, PADR, 256), jnp.bfloat16)],
        compiler_params=pltpu.CompilerParams(vmem_limit_bytes=58 << 20),
        name="section_factors",
    )(rf, select_matrices(), diagonal_mask(), first)


def butterfly_kernel(rx_ref, near_ref, far_ref, order_ref, out_ref, xa, xb, xc, xd):
    step = pl.program_id(0)

    @pl.when(step == 0)
    def _():
        for b in range(8):
            xa[b, pl.ds(96, 16), :] = jnp.zeros((16, PART), jnp.bfloat16)

    @pl.when(step < 4)
    def _():
        for b in range(8):
            xa[b, pl.ds(0, ROWS), :] = rx_ref[b]
        src, dst = xa, xb
        for s in range(3):
            base = 8 * step if s == 2 else 0
            out = xc if s == 2 else dst
            for j in range(4):
                low = lower_block(s, 0, j)
                high = low + (1 << s)
                right = jnp.concatenate([src[low], src[high]], axis=0)
                y = jnp.dot(near_ref[0, 4 * s + j], right, preferred_element_type=jnp.float32).astype(jnp.bfloat16)
                out[base + low] = y[:PADR]
                out[base + high] = y[PADR:]
            src, dst = dst, src

    @pl.when(step >= 4)
    def _():
        first = 2 * (step - 4)
        for j in range(4):
            r, h = j // 2, j % 2
            low = first + r + 16 * h
            right = jnp.concatenate([xc[low], xc[low + 8]], axis=0)
            y = jnp.dot(far_ref[0, j], right, preferred_element_type=jnp.float32).astype(jnp.bfloat16)
            xd[r, 2 * h] = y[:PADR]
            xd[r, 2 * h + 1] = y[PADR:]
        for j in range(4):
            r, h = j // 2, j % 2
            right = jnp.concatenate([xd[r, h], xd[r, h + 2]], axis=0)
            y = jnp.dot(far_ref[0, 4 + j], right, preferred_element_type=jnp.float32).astype(jnp.bfloat16)
            re = jnp.concatenate([y[:PADR, :HALF], y[PADR:, :HALF]], axis=1)
            im = jnp.concatenate([y[:PADR, HALF:], y[PADR:, HALF:]], axis=1)
            z = jnp.dot(order_ref[...], jnp.concatenate([re, im], axis=0), preferred_element_type=jnp.float32)
            for half in range(2):
                for band in range(BANDS):
                    piece = z[band * SLOT:(band + 1) * SLOT, half * HALF:(half + 1) * HALF]
                    out_ref[h + 2 * half, r, band] = piece.astype(jnp.bfloat16)


def butterfly_more_kernel(rx_ref, near_ref, far_ref, order_ref, rows_ref, out_ref, *scratch):
    butterfly_kernel(rx_ref, near_ref, far_ref, order_ref, out_ref, *scratch)


def butterfly(rx, lane_block, near, far, rows):
    early = lambda i: jnp.minimum(i, 3)
    late = lambda i: jnp.maximum(i - 4, 0)
    half = 0 if rows is None else 1
    return pl.pallas_call(
        butterfly_more_kernel if half else butterfly_kernel,
        out_shape=jax.ShapeDtypeStruct((4, 8, BANDS, SLOT, 2 * HALF), jnp.bfloat16),
        grid=(8,),
        in_specs=[
            pl.BlockSpec((8, ROWS, PART), lambda i: (early(i), 0, lane_block)),
            pl.BlockSpec((1, 12, PAIR, PAIR), lambda i: (early(i), 0, 0, 0)),
            pl.BlockSpec((1, 8, PAIR, PAIR), lambda i: (late(i), 0, 0, 0)),
            pl.BlockSpec((BANDS * SLOT, PAIR), lambda i: (0, 0)),
        ] + [pl.BlockSpec(memory_space=pl.ANY)] * half,
        out_specs=pl.BlockSpec((4, 2, BANDS, SLOT, HALF), lambda i: (0, late(i), 0, 0, half)),
        scratch_shapes=[
            pltpu.VMEM((8, PADR, PART), jnp.bfloat16),
            pltpu.VMEM((8, PADR, PART), jnp.bfloat16),
            pltpu.VMEM((BLOCKS, PADR, PART), jnp.bfloat16),
            pltpu.VMEM((2, 4, PADR, PART), jnp.bfloat16),
        ],
        input_output_aliases={4: 0} if half else {},
        compiler_params=pltpu.CompilerParams(vmem_limit_bytes=56 << 20),
        name="butterfly",
    )(rx, near, far, send_order(), *([rows] * half))


def mirror_order():
    row = lax.broadcasted_iota(jnp.int32, (256, 256), 0)
    lane = lax.broadcasted_iota(jnp.int32, (256, 256), 1)
    return (row + lane == 256).astype(jnp.bfloat16)


def fourier_kernel(u_ref, order_ref, mirror_ref, table_ref, middle_ref, out_ref, v, vt, edge, buf, sem):
    step = pl.program_id(0)
    slot = step % 2
    tile = 256

    def copies(at, into):
        near = pltpu.make_async_copy(buf.at[into, 0], out_ref.at[:, :, pl.ds((4 - at) * tile, tile)], sem.at[into, 0])
        far = pltpu.make_async_copy(buf.at[into, 1], out_ref.at[:, :, pl.ds((5 + at) * tile, tile)], sem.at[into, 1])
        return near, far

    def sums(table):
        even = jnp.dot(vt[:, :640], table[:640], preferred_element_type=jnp.float32)
        odd = jnp.dot(vt[:, 640:], table[640:], preferred_element_type=jnp.float32)
        return even, odd

    @pl.when(step == 0)
    def _():
        for g in range(16):
            piece = u_ref[pl.ds(8 * g, 8)].reshape(8 * SLOT, PART)
            y = jnp.dot(order_ref[...], piece, preferred_element_type=jnp.float32)
            for p in range(2):
                for r in range(5):
                    at = p * 200 + r * 40
                    v[r, pl.ds(p * 640 + 40 * g, 40), :] = y[at:at + 40].astype(jnp.bfloat16)
        for r in range(5):
            vt[pl.ds(r * PART, PART), :] = v[r].T
        even, odd = sums(middle_ref[...])
        edge[...] = even - odd

    @pl.when(step >= 2)
    def _():
        for copy in copies(step - 2, slot):
            copy.wait()

    even, odd = sums(table_ref[...])
    near = (even + odd).astype(jnp.bfloat16)
    far = (even - odd).astype(jnp.bfloat16)
    turned = jnp.dot(far, mirror_ref[...], preferred_element_type=jnp.float32)
    lane = lax.broadcasted_iota(jnp.int32, (5 * PART, 128), 1)
    head = jnp.where(lane == 0, edge[...], turned[:, :128]).astype(jnp.bfloat16)
    tail = turned[:, 128:].astype(jnp.bfloat16)
    edge[...] = far[:, :128].astype(jnp.float32)
    for r in range(5):
        rows = slice(r * PART, (r + 1) * PART)
        buf[slot, 0, r] = near[rows]
        buf[slot, 1, r, :, pl.ds(0, 128)] = head[rows]
        buf[slot, 1, r, :, pl.ds(128, 128)] = tail[rows]
    for copy in copies(step, slot):
        copy.start()

    @pl.when(step == 4)
    def _():
        for copy in copies(3, 1) + copies(4, 0):
            copy.wait()


def fourier(u, table):
    return pl.pallas_call(
        fourier_kernel,
        out_shape=jax.ShapeDtypeStruct((5, PART, NLON), jnp.bfloat16),
        grid=(5,),
        in_specs=[
            pl.BlockSpec((BLOCKS * BANDS, SLOT, PART), lambda j: (0, 0, 0)),
            pl.BlockSpec((400, 8 * SLOT), lambda j: (0, 0)),
            pl.BlockSpec((256, 256), lambda j: (0, 0)),
            pl.BlockSpec((1280, 256), lambda j: (0, 4 - j)),
            pl.BlockSpec((1280, 128), lambda j: (0, 10)),
        ],
        out_specs=pl.BlockSpec(memory_space=pl.ANY),
        scratch_shapes=[
            pltpu.VMEM((5, 1280, PART), jnp.bfloat16),
            pltpu.VMEM((5 * PART, 1280), jnp.bfloat16),
            pltpu.VMEM((5 * PART, 128), jnp.float32),
            pltpu.VMEM((2, 2, 5, PART, 256), jnp.bfloat16),
            pltpu.SemaphoreType.DMA((2, 2)),
        ],
        compiler_params=pltpu.CompilerParams(vmem_limit_bytes=60 << 20),
        name="fourier",
    )(u, receive_order(), mirror_order(), table, table)


def fourier_table(ids):
    longitude = jnp.arange(NLON // 2 + 128, dtype=jnp.int32)
    phases = ids[:, None] * longitude[None, :] % NLON
    angles = phases.astype(jnp.float32) * (2.0 * math.pi / NLON)
    weight = jnp.where(ids == 0, 1.0, 2.0).astype(jnp.float32) / math.sqrt(2.0 * ids.shape[0])
    cosine_part = weight[:, None] * jnp.cos(angles)
    sine_part = -weight[:, None] * jnp.sin(angles)
    return jnp.concatenate([cosine_part, sine_part], axis=0).astype(jnp.bfloat16)


def body(coefficients, factors, wave_ids):
    wave_pos = lax.axis_index("wave")
    lev_pos = lax.axis_index("lev")
    rx0 = lax.all_to_all(pack_first(factors, coefficients), "wave", 0, 0, tiled=True)
    send1, rx0 = lax.optimization_barrier((pack_second(coefficients), rx0))
    rx1 = lax.all_to_all(send1, "wave", 0, 0, tiled=True)
    own_ids = lax.dynamic_slice_in_dim(wave_ids, lev_pos * (OWN * BLOCKS) + wave_pos * OWN, OWN, 0)
    first = (own_ids[:, None] - jnp.arange(DEG, dtype=jnp.int32)[None, :]).reshape(ROWS)
    first = jnp.pad(first, (0, PADR - ROWS))
    first = jnp.broadcast_to(jnp.concatenate([first, first])[None, :], (8, PAIR))
    near, far = section_factors(rx0, first)
    rows = butterfly(rx0, 1, near, far, None)
    rows, rx1 = lax.optimization_barrier((rows, rx1))
    rows = butterfly(rx1, 0, near, far, rows).reshape(BLOCKS * BANDS, SLOT, 2 * HALF)
    u = lax.all_to_all(rows, ("wave", "lev"), 0, 0, tiled=True)
    ids = wave_ids.reshape(BANDS, BLOCKS, OWN).transpose(1, 0, 2).reshape(-1)
    return fourier(u, fourier_table(ids))


def solution(mesh):
    in_specs = (P("wave", "lev", None), P(None, None, "wave", None, "lev"), P())
    out_specs = P(("wave", "lev"), None, None)
    return jax.shard_map(body, mesh=mesh, in_specs=in_specs, out_specs=out_specs, check_vma=False)
```

```python
import functools
import math

import jax
import jax.numpy as jnp
import numpy as np
from jax import lax
from jax.experimental import pallas as pl
from jax.experimental.pallas import tpu as pltpu
from jax.sharding import PartitionSpec as P

NLON = 2560
SECTIONS = 5
BLOCKS = 32
BANDS = 4
DEG = 20
OWN = 5
CH = 512
PART = 256
HALF = 128
ROWS = DEG * OWN
PADR = 112
SLOT = 56
PAIR = 2 * PADR


def select_matrices():
    shape = (SECTIONS, 2, 256, PAIR)
    s, v, q, lane = (lax.broadcasted_iota(jnp.int32, shape, d) for d in range(4))
    part = (lane // PADR) ^ v
    inner = lane % PADR
    hit = (q == s * 40 + (inner % DEG) * 2 + part) & (inner < ROWS)
    return hit.astype(jnp.bfloat16)


def diagonal_mask():
    row = lax.broadcasted_iota(jnp.int32, (PADR, PAIR), 0)
    inner = lax.broadcasted_iota(jnp.int32, (PADR, PAIR), 1) % PADR
    hit = (row // DEG == inner // DEG) & (row < ROWS) & (inner < ROWS)
    return hit.astype(jnp.float32)


def send_order():
    row = lax.broadcasted_iota(jnp.int32, (BANDS * SLOT, PAIR), 0)
    col = lax.broadcasted_iota(jnp.int32, (BANDS * SLOT, PAIR), 1)
    band, inner = row // SLOT, row % SLOT
    part, kr = inner // 25, inner % 25
    want = part * PADR + (kr // 5) * DEG + 5 * band + kr % 5
    return ((col == want) & (inner < 50)).astype(jnp.bfloat16)


def fill_pack_order(order):
    shape = (4 * 104, DEG * 32)
    row = lax.broadcasted_iota(jnp.int32, shape, 0)
    col = lax.broadcasted_iota(jnp.int32, shape, 1)
    owner = (row >= 104).astype(jnp.int32) + (row >= 208).astype(jnp.int32) + (row >= 312).astype(jnp.int32)
    inner = row - 104 * owner
    k = sum((inner >= DEG * i).astype(jnp.int32) for i in range(1, OWN))
    base = (inner - DEG * k) * 32 + OWN * owner + k
    ahead = jnp.where(inner < ROWS, col - base, -1)
    for v in range(4):
        order[v] = (ahead == 4 * v).astype(jnp.float32).astype(jnp.bfloat16)


def pack_rows(srcs, order, out_ref):
    for group in range(BLOCKS // 4):
        start = 4 * OWN * group
        at = start // 16 * 16
        window = jnp.concatenate([src[:, at:at + 32, :].reshape(DEG * 32, src.shape[2]) for src in srcs], axis=1)
        y = jnp.dot(order[(start - at) // 4], window, preferred_element_type=jnp.float32)
        for d in range(4):
            out_ref[4 * group + d] = y[104 * d:104 * d + ROWS].astype(jnp.bfloat16)


def pack_first_kernel(f_ref, eye_ref, x_ref, out_ref, turned, order, xs, sem):
    fetch = [
        pltpu.make_async_copy(x_ref.at[:, :, pl.ds(p * PART, HALF)], xs.at[:, :, pl.ds(p * HALF, HALF)], sem.at[p])
        for p in range(2)
    ]

    @pl.when(pl.program_id(0) == 0)
    def _():
        for copy in fetch:
            copy.start()
        fill_pack_order(order)
        for o in range(DEG):
            left = jnp.concatenate([f_ref[s, o].reshape(2 * DEG, OWN * BLOCKS) for s in range(SECTIONS)], axis=0)
            y = lax.dot_general(left, eye_ref[...], (((0,), (0,)), ((), ())), preferred_element_type=jnp.float32)
            turned[o] = y.astype(jnp.bfloat16)
        pack_rows([turned], order, out_ref)

    @pl.when(pl.program_id(0) == 1)
    def _():
        for copy in fetch:
            copy.wait()
        pack_rows([xs], order, out_ref)


def pack_first(factors, x):
    return pl.pallas_call(
        pack_first_kernel,
        out_shape=jax.ShapeDtypeStruct((BLOCKS, ROWS, 2 * PART), jnp.bfloat16),
        grid=(2,),
        in_specs=[
            pl.BlockSpec((SECTIONS, DEG, DEG, 2, OWN * BLOCKS), lambda i: (0, 0, 0, 0, 0)),
            pl.BlockSpec((200, 256), lambda i: (0, 0)),
            pl.BlockSpec(memory_space=pl.ANY),
        ],
        out_specs=pl.BlockSpec((BLOCKS, ROWS, PART), lambda i: (0, 0, i)),
        scratch_shapes=[
            pltpu.VMEM((DEG, OWN * BLOCKS, 256), jnp.bfloat16),
            pltpu.VMEM((4, 416, 640), jnp.bfloat16),
            pltpu.VMEM((DEG, OWN * BLOCKS, PART), jnp.bfloat16),
            pltpu.SemaphoreType.DMA((2,)),
        ],
        compiler_params=pltpu.CompilerParams(vmem_limit_bytes=60 << 20),
        name="pack_first",
    )(factors.transpose(0, 2, 3, 1, 4), jnp.asarray(np.eye(200, 256), jnp.bfloat16), x)


def pack_second_kernel(re_ref, im_ref, out_ref, order):
    fill_pack_order(order)
    pack_rows([re_ref, im_ref], order, out_ref)


def pack_second(x):
    return pl.pallas_call(
        pack_second_kernel,
        out_shape=jax.ShapeDtypeStruct((BLOCKS, ROWS, PART), jnp.bfloat16),
        grid=(1,),
        in_specs=[
            pl.BlockSpec((DEG, OWN * BLOCKS, HALF), lambda i: (0, 0, 1)),
            pl.BlockSpec((DEG, OWN * BLOCKS, HALF), lambda i: (0, 0, 3)),
        ],
        out_specs=pl.BlockSpec((BLOCKS, ROWS, PART), lambda i: (0, 0, 0)),
        scratch_shapes=[pltpu.VMEM((4, 416, 640), jnp.bfloat16)],
        compiler_params=pltpu.CompilerParams(vmem_limit_bytes=60 << 20),
        name="pack_second",
    )(x, x)


def receive_order():
    row = lax.broadcasted_iota(jnp.int32, (400, 8 * SLOT), 0)
    col = lax.broadcasted_iota(jnp.int32, (400, 8 * SLOT), 1)
    part, lat = row // 200, (row // 40) % 5
    src, k = (row % 40) // 5, row % 5
    return (col == src * SLOT + part * 25 + k * 5 + lat).astype(jnp.bfloat16)


def lower_block(s, group, j):
    if s < 3:
        return 8 * group + (j >> s) * (2 << s) + (j & ((1 << s) - 1))
    step = 16 if s == 3 else 8
    return 2 * group + j // 2 + step * (j % 2)


def section_kernel(rf_ref, e_ref, mask_ref, first_ref, near_ref, far_ref, fc):
    zeros_f = jnp.zeros((16, 256), jnp.bfloat16)

    def load(b, carry):
        fc[b, pl.ds(96, 16), :] = zeros_f
        fc[b, pl.ds(0, ROWS), :] = rf_ref[b]
        return carry

    lax.fori_loop(0, BLOCKS, load, 0)
    lane_high = lax.broadcasted_iota(jnp.int32, (8, PAIR), 1) // PADR
    mask = mask_ref[...]
    for s in range(SECTIONS):
        lows = [(g, j, lower_block(s, g, j)) for g in range(4) for j in range(4)]
        for v in range(2):
            left = jnp.concatenate([fc[low + (v << s)] for _, _, low in lows], axis=0)
            f = jnp.dot(left, e_ref[s, v], preferred_element_type=jnp.float32)
            for i, (g, j, low) in enumerate(lows):
                keep = mask
                if s == 0:
                    start = DEG * (low + lane_high)
                    live = (start >= first_ref[...]).astype(jnp.float32)
                    keep = mask * live[0:1, :]
                piece = (f[i * PADR:(i + 1) * PADR] * keep).astype(jnp.bfloat16)
                if s < 3:
                    near_ref[g, 4 * s + j, pl.ds(v * PADR, PADR), :] = piece
                else:
                    far_ref[g, 4 * (s - 3) + j, pl.ds(v * PADR, PADR), :] = piece


def section_factors(rf, first):
    return pl.pallas_call(
        section_kernel,
        out_shape=[
            jax.ShapeDtypeStruct((4, 12, PAIR, PAIR), jnp.bfloat16),
            jax.ShapeDtypeStruct((4, 8, PAIR, PAIR), jnp.bfloat16),
        ],
        grid=(1,),
        in_specs=[
            pl.BlockSpec((BLOCKS, ROWS, 256), lambda i: (0, 0, 0)),
            pl.BlockSpec((SECTIONS, 2, 256, PAIR), lambda i: (0, 0, 0, 0)),
            pl.BlockSpec((PADR, PAIR), lambda i: (0, 0)),
            pl.BlockSpec((8, PAIR), lambda i: (0, 0)),
        ],
        out_specs=[
            pl.BlockSpec((4, 12, PAIR, PAIR), lambda i: (0, 0, 0, 0)),
            pl.BlockSpec((4, 8, PAIR, PAIR), lambda i: (0, 0, 0, 0)),
        ],
        scratch_shapes=[pltpu.VMEM((BLOCKS, PADR, 256), jnp.bfloat16)],
        compiler_params=pltpu.CompilerParams(vmem_limit_bytes=58 << 20),
        name="section_factors",
    )(rf, select_matrices(), diagonal_mask(), first)


def butterfly_kernel(half, lane_block, rx_ref, near_ref, far_ref, order_ref, *refs):
    out_ref, rs, ns, fs, stage, xa, xb, xc, xd, rsem, nsem, fsem, osem = refs[-13:]

    def load_rows(g):
        rows = rx_ref.at[pl.ds(8 * g, 8), :, pl.ds(PART * lane_block, PART)]
        return pltpu.make_async_copy(rows, rs.at[pl.ds(8 * g, 8)], rsem.at[g])

    def load_near(g, s):
        return pltpu.make_async_copy(near_ref.at[g, pl.ds(4 * s, 4)], ns.at[g, pl.ds(4 * s, 4)], nsem.at[g, s])

    def load_far(t):
        return pltpu.make_async_copy(far_ref.at[t], fs.at[t], fsem.at[t])

    def store(t):
        rows = out_ref.at[:, pl.ds(2 * t, 2), :, :, pl.ds(HALF * half, HALF)]
        return pltpu.make_async_copy(stage.at[:, pl.ds(2 * t, 2)], rows, osem.at[t])

    for g in range(4):
        load_rows(g).start()
        for s in range(3):
            load_near(g, s).start()
    for t in range(4):
        load_far(t).start()
    for b in range(16):
        xa[b, pl.ds(96, 16), :] = jnp.zeros((16, PART), jnp.bfloat16)

    def early(i, carry):
        for q in range(2):
            load_rows(2 * i + q).wait()
            for b in range(8):
                xa[8 * q + b, pl.ds(0, ROWS), :] = rs[16 * i + 8 * q + b]
        src, dst = xa, xb
        for s in range(3):
            base = 16 * i if s == 2 else 0
            out = xc if s == 2 else dst
            for q in range(2):
                load_near(2 * i + q, s).wait()
            for q in range(2):
                for j in range(4):
                    low = lower_block(s, q, j)
                    high = low + (1 << s)
                    right = jnp.concatenate([src[low], src[high]], axis=0)
                    y = jnp.dot(ns[2 * i + q, 4 * s + j], right, preferred_element_type=jnp.float32)
                    y = y.astype(jnp.bfloat16)
                    out[base + low] = y[:PADR]
                    out[base + high] = y[PADR:]
            src, dst = dst, src
        return carry

    lax.fori_loop(0, 2, early, 0)

    def late(i, carry):
        for q in range(2):
            load_far(2 * i + q).wait()
        for q in range(2):
            for j in range(4):
                r, h = j // 2, j % 2
                low = 4 * i + 2 * q + r + 16 * h
                right = jnp.concatenate([xc[low], xc[low + 8]], axis=0)
                y = jnp.dot(fs[2 * i + q, j], right, preferred_element_type=jnp.float32).astype(jnp.bfloat16)
                xd[2 * q + r, 2 * h] = y[:PADR]
                xd[2 * q + r, 2 * h + 1] = y[PADR:]
        for q in range(2):
            for j in range(4):
                r, h = j // 2, j % 2
                right = jnp.concatenate([xd[2 * q + r, h], xd[2 * q + r, h + 2]], axis=0)
                y = jnp.dot(fs[2 * i + q, 4 + j], right, preferred_element_type=jnp.float32).astype(jnp.bfloat16)
                re = jnp.concatenate([y[:PADR, :HALF], y[PADR:, :HALF]], axis=1)
                im = jnp.concatenate([y[:PADR, HALF:], y[PADR:, HALF:]], axis=1)
                z = jnp.dot(order_ref[...], jnp.concatenate([re, im], axis=0), preferred_element_type=jnp.float32)
                for k in range(2):
                    for band in range(BANDS):
                        piece = z[band * SLOT:(band + 1) * SLOT, k * HALF:(k + 1) * HALF]
                        stage[h + 2 * k, 4 * i + 2 * q + r, band] = piece.astype(jnp.bfloat16)
            store(2 * i + q).start()
        return carry

    lax.fori_loop(0, 2, late, 0)
    for t in range(4):
        store(t).wait()


def butterfly(rx, lane_block, near, far, rows):
    half = 0 if rows is None else 1
    anywhere = pl.BlockSpec(memory_space=pl.ANY)
    return pl.pallas_call(
        functools.partial(butterfly_kernel, half, lane_block),
        out_shape=jax.ShapeDtypeStruct((4, 8, BANDS, SLOT, 2 * HALF), jnp.bfloat16),
        in_specs=[anywhere, anywhere, anywhere, pl.BlockSpec(memory_space=pltpu.VMEM)] + [anywhere] * half,
        out_specs=anywhere,
        scratch_shapes=[
            pltpu.VMEM((BLOCKS, ROWS, PART), jnp.bfloat16),
            pltpu.VMEM((4, 12, PAIR, PAIR), jnp.bfloat16),
            pltpu.VMEM((4, 8, PAIR, PAIR), jnp.bfloat16),
            pltpu.VMEM((4, 8, BANDS, SLOT, HALF), jnp.bfloat16),
            pltpu.VMEM((16, PADR, PART), jnp.bfloat16),
            pltpu.VMEM((16, PADR, PART), jnp.bfloat16),
            pltpu.VMEM((BLOCKS, PADR, PART), jnp.bfloat16),
            pltpu.VMEM((4, 4, PADR, PART), jnp.bfloat16),
            pltpu.SemaphoreType.DMA((4,)),
            pltpu.SemaphoreType.DMA((4, 3)),
            pltpu.SemaphoreType.DMA((4,)),
            pltpu.SemaphoreType.DMA((4,)),
        ],
        input_output_aliases={4: 0} if half else {},
        compiler_params=pltpu.CompilerParams(vmem_limit_bytes=56 << 20),
        name="butterfly",
    )(rx, near, far, send_order(), *([rows] * half))


def mirror_order():
    row = lax.broadcasted_iota(jnp.int32, (256, 256), 0)
    lane = lax.broadcasted_iota(jnp.int32, (256, 256), 1)
    return (row + lane == 256).astype(jnp.bfloat16)


def fourier_kernel(u_ref, order_ref, mirror_ref, table_ref, middle_ref, out_ref, v, vt, edge, buf, sem):
    step = pl.program_id(0)
    slot = step % 2
    tile = 256

    def copies(at, into):
        near = pltpu.make_async_copy(buf.at[into, 0], out_ref.at[:, :, pl.ds((4 - at) * tile, tile)], sem.at[into, 0])
        far = pltpu.make_async_copy(buf.at[into, 1], out_ref.at[:, :, pl.ds((5 + at) * tile, tile)], sem.at[into, 1])
        return near, far

    def sums(table):
        even = jnp.dot(vt[:, :640], table[:640], preferred_element_type=jnp.float32)
        odd = jnp.dot(vt[:, 640:], table[640:], preferred_element_type=jnp.float32)
        return even, odd

    @pl.when(step == 0)
    def _():
        for g in range(16):
            piece = u_ref[pl.ds(8 * g, 8)].reshape(8 * SLOT, PART)
            y = jnp.dot(order_ref[...], piece, preferred_element_type=jnp.float32)
            for p in range(2):
                for r in range(5):
                    at = p * 200 + r * 40
                    v[r, pl.ds(p * 640 + 40 * g, 40), :] = y[at:at + 40].astype(jnp.bfloat16)
        for r in range(5):
            vt[pl.ds(r * PART, PART), :] = v[r].T
        even, odd = sums(middle_ref[...])
        edge[...] = even - odd

    @pl.when(step >= 2)
    def _():
        for copy in copies(step - 2, slot):
            copy.wait()

    even, odd = sums(table_ref[...])
    near = (even + odd).astype(jnp.bfloat16)
    far = (even - odd).astype(jnp.bfloat16)
    turned = jnp.dot(far, mirror_ref[...], preferred_element_type=jnp.float32)
    lane = lax.broadcasted_iota(jnp.int32, (5 * PART, 128), 1)
    head = jnp.where(lane == 0, edge[...], turned[:, :128]).astype(jnp.bfloat16)
    tail = turned[:, 128:].astype(jnp.bfloat16)
    edge[...] = far[:, :128].astype(jnp.float32)
    for r in range(5):
        rows = slice(r * PART, (r + 1) * PART)
        buf[slot, 0, r] = near[rows]
        buf[slot, 1, r, :, pl.ds(0, 128)] = head[rows]
        buf[slot, 1, r, :, pl.ds(128, 128)] = tail[rows]
    for copy in copies(step, slot):
        copy.start()

    @pl.when(step == 4)
    def _():
        for copy in copies(3, 1) + copies(4, 0):
            copy.wait()


def fourier(u, table):
    return pl.pallas_call(
        fourier_kernel,
        out_shape=jax.ShapeDtypeStruct((5, PART, NLON), jnp.bfloat16),
        grid=(5,),
        in_specs=[
            pl.BlockSpec((BLOCKS * BANDS, SLOT, PART), lambda j: (0, 0, 0)),
            pl.BlockSpec((400, 8 * SLOT), lambda j: (0, 0)),
            pl.BlockSpec((256, 256), lambda j: (0, 0)),
            pl.BlockSpec((1280, 256), lambda j: (0, 4 - j)),
            pl.BlockSpec((1280, 128), lambda j: (0, 10)),
        ],
        out_specs=pl.BlockSpec(memory_space=pl.ANY),
        scratch_shapes=[
            pltpu.VMEM((5, 1280, PART), jnp.bfloat16),
            pltpu.VMEM((5 * PART, 1280), jnp.bfloat16),
            pltpu.VMEM((5 * PART, 128), jnp.float32),
            pltpu.VMEM((2, 2, 5, PART, 256), jnp.bfloat16),
            pltpu.SemaphoreType.DMA((2, 2)),
        ],
        compiler_params=pltpu.CompilerParams(vmem_limit_bytes=60 << 20),
        name="fourier",
    )(u, receive_order(), mirror_order(), table, table)


def fourier_table(ids):
    longitude = jnp.arange(NLON // 2 + 128, dtype=jnp.int32)
    phases = ids[:, None] * longitude[None, :] % NLON
    angles = phases.astype(jnp.float32) * (2.0 * math.pi / NLON)
    weight = jnp.where(ids == 0, 1.0, 2.0).astype(jnp.float32) / math.sqrt(2.0 * ids.shape[0])
    cosine_part = weight[:, None] * jnp.cos(angles)
    sine_part = -weight[:, None] * jnp.sin(angles)
    return jnp.concatenate([cosine_part, sine_part], axis=0).astype(jnp.bfloat16)


def body(coefficients, factors, wave_ids):
    wave_pos = lax.axis_index("wave")
    lev_pos = lax.axis_index("lev")
    rx0 = lax.all_to_all(pack_first(factors, coefficients), "wave", 0, 0, tiled=True)
    send1, rx0 = lax.optimization_barrier((pack_second(coefficients), rx0))
    rx1 = lax.all_to_all(send1, "wave", 0, 0, tiled=True)
    own_ids = lax.dynamic_slice_in_dim(wave_ids, lev_pos * (OWN * BLOCKS) + wave_pos * OWN, OWN, 0)
    first = (own_ids[:, None] - jnp.arange(DEG, dtype=jnp.int32)[None, :]).reshape(ROWS)
    first = jnp.pad(first, (0, PADR - ROWS))
    first = jnp.broadcast_to(jnp.concatenate([first, first])[None, :], (8, PAIR))
    near, far = section_factors(rx0, first)
    rows = butterfly(rx0, 1, near, far, None)
    rows, rx1 = lax.optimization_barrier((rows, rx1))
    rows = butterfly(rx1, 0, near, far, rows).reshape(BLOCKS * BANDS, SLOT, 2 * HALF)
    u = lax.all_to_all(rows, ("wave", "lev"), 0, 0, tiled=True)
    ids = wave_ids.reshape(BANDS, BLOCKS, OWN).transpose(1, 0, 2).reshape(-1)
    return fourier(u, fourier_table(ids))


def solution(mesh):
    in_specs = (P("wave", "lev", None), P(None, None, "wave", None, "lev"), P())
    out_specs = P(("wave", "lev"), None, None)
    return jax.shard_map(body, mesh=mesh, in_specs=in_specs, out_specs=out_specs, check_vma=False)
```

```python
import functools
import math

import jax
import jax.numpy as jnp
import numpy as np
from jax import lax
from jax.experimental import pallas as pl
from jax.experimental.pallas import tpu as pltpu
from jax.sharding import PartitionSpec as P

NLON = 2560
SECTIONS = 5
BLOCKS = 32
BANDS = 4
DEG = 20
OWN = 5
CH = 512
PART = 256
HALF = 128
ROWS = DEG * OWN
PADR = 112
SLOT = 56
PAIR = 2 * PADR
XROWS = 104
FROWS = 80


def select_matrices():
    shape = (SECTIONS, 2, 256, PAIR)
    s, v, q, lane = (lax.broadcasted_iota(jnp.int32, shape, d) for d in range(4))
    part = (lane // PADR) ^ v
    inner = lane % PADR
    hit = (q == s * 40 + (inner % DEG) * 2 + part) & (inner < ROWS)
    return hit.astype(jnp.bfloat16)


def diagonal_mask():
    row = lax.broadcasted_iota(jnp.int32, (PADR, PAIR), 0)
    inner = lax.broadcasted_iota(jnp.int32, (PADR, PAIR), 1) % PADR
    hit = (row // DEG == inner // DEG) & (row < ROWS) & (inner < ROWS)
    return hit.astype(jnp.float32)


def send_order():
    row = lax.broadcasted_iota(jnp.int32, (BANDS * SLOT, PAIR), 0)
    col = lax.broadcasted_iota(jnp.int32, (BANDS * SLOT, PAIR), 1)
    band, inner = row // SLOT, row % SLOT
    part, kr = inner // 25, inner % 25
    want = part * PADR + (kr // 5) * DEG + 5 * band + kr % 5
    return ((col == want) & (inner < 50)).astype(jnp.bfloat16)


def fill_pack_order(order):
    shape = (4 * 104, DEG * 32)
    row = lax.broadcasted_iota(jnp.int32, shape, 0)
    col = lax.broadcasted_iota(jnp.int32, shape, 1)
    owner = (row >= 104).astype(jnp.int32) + (row >= 208).astype(jnp.int32) + (row >= 312).astype(jnp.int32)
    inner = row - 104 * owner
    k = sum((inner >= DEG * i).astype(jnp.int32) for i in range(1, OWN))
    base = (inner - DEG * k) * 32 + OWN * owner + k
    ahead = jnp.where(inner < ROWS, col - base, -1)
    for v in range(4):
        order[v] = (ahead == 4 * v).astype(jnp.float32).astype(jnp.bfloat16)


def fold_lanes():
    f = np.zeros((256, 512), np.float32)
    for q in range(4):
        for j in range(50):
            f[50 * q + j, 128 * q + 72 + j] = 1
    return f


def fold_rows():
    f = np.zeros((FROWS, 96), np.float32)
    for q in range(4):
        for o in range(DEG):
            row = 16 * q + o if o < 16 else 64 + 4 * q + o - 16
            f[row, 24 * q + o] = 1
    return f


def chosen_rows(srcs, order, group):
    start = 4 * OWN * group
    at = start // 16 * 16
    window = jnp.concatenate([src[:, at:at + 32, :].reshape(DEG * 32, src.shape[2]) for src in srcs], axis=1)
    return jnp.dot(order[(start - at) // 4], window, preferred_element_type=jnp.float32)


def pack_rows(srcs, order, out_ref, first):
    for group in range(BLOCKS // 4):
        y = chosen_rows(srcs, order, group)
        for d in range(4):
            out_ref[4 * group + d, pl.ds(first, XROWS), :] = y[XROWS * d:XROWS * (d + 1)].astype(jnp.bfloat16)


def pack_folded(src, order, lanes_ref, out_ref):
    for group in range(BLOCKS // 4):
        y = chosen_rows([src], order, group)
        rest = [y[XROWS * d + FROWS:XROWS * (d + 1)].astype(jnp.bfloat16) for d in range(4)]
        wide = jnp.dot(jnp.concatenate(rest, axis=0), lanes_ref[...], preferred_element_type=jnp.float32)
        for d in range(4):
            part = [wide[24 * d:24 * (d + 1), 128 * q:128 * (q + 1)] for q in range(4)]
            ends = [part[q][16:] + pltpu.roll(part[q + 1][16:], 4, 0) for q in (0, 2)]
            spare = jnp.concatenate([part[q][:16] for q in range(4)] + ends, axis=0)
            own = y[XROWS * d:XROWS * d + FROWS]
            out_ref[4 * group + d, pl.ds(0, FROWS), pl.ds(0, 128)] = own[:, :128].astype(jnp.bfloat16)
            out_ref[4 * group + d, pl.ds(0, FROWS), pl.ds(128, 128)] = (own[:, 128:] + spare).astype(jnp.bfloat16)


def pack_first_kernel(f_ref, eye_ref, lanes_ref, x_ref, out_ref, turned, order, xs, stage, sem, osem):
    fetch = [
        pltpu.make_async_copy(x_ref.at[:, :, pl.ds(p * PART, HALF)], xs.at[:, :, pl.ds(p * HALF, HALF)], sem.at[p])
        for p in range(2)
    ]
    for copy in fetch:
        copy.start()
    fill_pack_order(order)
    for o in range(DEG):
        left = jnp.concatenate([f_ref[s, o].reshape(2 * DEG, OWN * BLOCKS) for s in range(SECTIONS)], axis=0)
        y = lax.dot_general(left, eye_ref[...], (((0,), (0,)), ((), ())), preferred_element_type=jnp.float32)
        turned[o] = y.astype(jnp.bfloat16)
    pack_folded(turned, order, lanes_ref, stage)
    pieces = [pl.ds(0, FROWS), pl.ds(FROWS, XROWS)]
    store = [pltpu.make_async_copy(stage.at[:, at, :], out_ref.at[:, at, :], osem.at[i]) for i, at in enumerate(pieces)]
    store[0].start()
    for copy in fetch:
        copy.wait()
    pack_rows([xs], order, stage, FROWS)
    store[1].start()
    for copy in store:
        copy.wait()


def pack_first(factors, x):
    here = pl.BlockSpec(memory_space=pltpu.VMEM)
    return pl.pallas_call(
        pack_first_kernel,
        out_shape=jax.ShapeDtypeStruct((BLOCKS, FROWS + XROWS, PART), jnp.bfloat16),
        in_specs=[here, here, here, pl.BlockSpec(memory_space=pl.ANY)],
        out_specs=pl.BlockSpec(memory_space=pl.ANY),
        scratch_shapes=[
            pltpu.VMEM((DEG, OWN * BLOCKS, 256), jnp.bfloat16),
            pltpu.VMEM((4, 416, 640), jnp.bfloat16),
            pltpu.VMEM((DEG, OWN * BLOCKS, PART), jnp.bfloat16),
            pltpu.VMEM((BLOCKS, FROWS + XROWS, PART), jnp.bfloat16),
            pltpu.SemaphoreType.DMA((2,)),
            pltpu.SemaphoreType.DMA((2,)),
        ],
        compiler_params=pltpu.CompilerParams(vmem_limit_bytes=60 << 20),
        name="pack_first",
    )(
        factors.transpose(0, 2, 3, 1, 4),
        jnp.asarray(np.eye(200, 256), jnp.bfloat16),
        jnp.asarray(fold_lanes(), jnp.bfloat16),
        x,
    )


def pack_second_kernel(re_ref, im_ref, out_ref, order):
    fill_pack_order(order)
    pack_rows([re_ref, im_ref], order, out_ref, 0)


def pack_second(x):
    return pl.pallas_call(
        pack_second_kernel,
        out_shape=jax.ShapeDtypeStruct((BLOCKS, XROWS, PART), jnp.bfloat16),
        grid=(1,),
        in_specs=[
            pl.BlockSpec((DEG, OWN * BLOCKS, HALF), lambda i: (0, 0, 1)),
            pl.BlockSpec((DEG, OWN * BLOCKS, HALF), lambda i: (0, 0, 3)),
        ],
        out_specs=pl.BlockSpec((BLOCKS, XROWS, PART), lambda i: (0, 0, 0)),
        scratch_shapes=[pltpu.VMEM((4, 416, 640), jnp.bfloat16)],
        compiler_params=pltpu.CompilerParams(vmem_limit_bytes=60 << 20),
        name="pack_second",
    )(x, x)


def receive_order():
    row = lax.broadcasted_iota(jnp.int32, (400, 8 * SLOT), 0)
    col = lax.broadcasted_iota(jnp.int32, (400, 8 * SLOT), 1)
    part, lat = row // 200, (row // 40) % 5
    src, k = (row % 40) // 5, row % 5
    return (col == src * SLOT + part * 25 + k * 5 + lat).astype(jnp.bfloat16)


def lower_block(s, group, j):
    if s < 3:
        return 8 * group + (j >> s) * (2 << s) + (j & ((1 << s) - 1))
    step = 16 if s == 3 else 8
    return 2 * group + j // 2 + step * (j % 2)


def section_kernel(rf_ref, e_ref, mask_ref, first_ref, lanes_ref, rows_ref, near_ref, far_ref, fc):
    zeros_f = jnp.zeros((16, 256), jnp.bfloat16)
    rest = []
    for b in range(BLOCKS):
        fc[b, pl.ds(96, 16), :] = zeros_f
        fc[b, pl.ds(0, FROWS), :] = rf_ref[b]
        tall = jnp.dot(rows_ref[...], rf_ref[b, :, 128:], preferred_element_type=jnp.float32)
        rest.append(jnp.concatenate([tall[24 * q:24 * (q + 1)] for q in range(4)], axis=1))
    rest = jnp.concatenate(rest, axis=0).astype(jnp.bfloat16)
    rest = jnp.dot(rest, lanes_ref[...], preferred_element_type=jnp.float32)
    for b in range(BLOCKS):
        fc[b, pl.ds(FROWS, 24), :] = rest[24 * b:24 * (b + 1)].astype(jnp.bfloat16)
    lane_high = lax.broadcasted_iota(jnp.int32, (8, PAIR), 1) // PADR
    mask = mask_ref[...]
    for s in range(SECTIONS):
        lows = [(g, j, lower_block(s, g, j)) for g in range(4) for j in range(4)]
        for v in range(2):
            left = jnp.concatenate([fc[low + (v << s)] for _, _, low in lows], axis=0)
            f = jnp.dot(left, e_ref[s, v], preferred_element_type=jnp.float32)
            for i, (g, j, low) in enumerate(lows):
                keep = mask
                if s == 0:
                    start = DEG * (low + lane_high)
                    live = (start >= first_ref[...]).astype(jnp.float32)
                    keep = mask * live[0:1, :]
                piece = (f[i * PADR:(i + 1) * PADR] * keep).astype(jnp.bfloat16)
                if s < 3:
                    near_ref[g, 4 * s + j, pl.ds(v * PADR, PADR), :] = piece
                else:
                    far_ref[g, 4 * (s - 3) + j, pl.ds(v * PADR, PADR), :] = piece


def section_factors(rf, first):
    return pl.pallas_call(
        section_kernel,
        out_shape=[
            jax.ShapeDtypeStruct((4, 12, PAIR, PAIR), jnp.bfloat16),
            jax.ShapeDtypeStruct((4, 8, PAIR, PAIR), jnp.bfloat16),
        ],
        grid=(1,),
        in_specs=[
            pl.BlockSpec((BLOCKS, FROWS, 256), lambda i: (0, 0, 0)),
            pl.BlockSpec((SECTIONS, 2, 256, PAIR), lambda i: (0, 0, 0, 0)),
            pl.BlockSpec((PADR, PAIR), lambda i: (0, 0)),
            pl.BlockSpec((8, PAIR), lambda i: (0, 0)),
            pl.BlockSpec((512, 256), lambda i: (0, 0)),
            pl.BlockSpec((96, FROWS), lambda i: (0, 0)),
        ],
        out_specs=[
            pl.BlockSpec((4, 12, PAIR, PAIR), lambda i: (0, 0, 0, 0)),
            pl.BlockSpec((4, 8, PAIR, PAIR), lambda i: (0, 0, 0, 0)),
        ],
        scratch_shapes=[pltpu.VMEM((BLOCKS, PADR, 256), jnp.bfloat16)],
        compiler_params=pltpu.CompilerParams(vmem_limit_bytes=58 << 20),
        name="section_factors",
    )(
        rf, select_matrices(), diagonal_mask(), first,
        jnp.asarray(fold_lanes().T, jnp.bfloat16), jnp.asarray(fold_rows().T, jnp.bfloat16),
    )


def butterfly_kernel(half, first_row, rx_ref, near_ref, far_ref, order_ref, *refs):
    out_ref, rs, ns, fs, stage, xa, xb, xc, xd, rsem, nsem, fsem, osem = refs[-13:]

    def load_rows(g):
        rows = rx_ref.at[pl.ds(8 * g, 8), pl.ds(first_row, XROWS), :]
        return pltpu.make_async_copy(rows, rs.at[pl.ds(8 * g, 8)], rsem.at[g])

    def load_near(g, s):
        return pltpu.make_async_copy(near_ref.at[g, pl.ds(4 * s, 4)], ns.at[g, pl.ds(4 * s, 4)], nsem.at[g, s])

    def load_far(t):
        return pltpu.make_async_copy(far_ref.at[t], fs.at[t], fsem.at[t])

    def store(t):
        rows = out_ref.at[:, pl.ds(2 * t, 2), :, :, pl.ds(HALF * half, HALF)]
        return pltpu.make_async_copy(stage.at[:, pl.ds(2 * t, 2)], rows, osem.at[t])

    for g in range(4):
        load_rows(g).start()
        for s in range(3):
            load_near(g, s).start()
    for t in range(4):
        load_far(t).start()
    for b in range(16):
        xa[b, pl.ds(96, 16), :] = jnp.zeros((16, PART), jnp.bfloat16)

    def early(i, carry):
        for q in range(2):
            load_rows(2 * i + q).wait()
            for b in range(8):
                xa[8 * q + b, pl.ds(0, XROWS), :] = rs[16 * i + 8 * q + b]
        src, dst = xa, xb
        for s in range(3):
            base = 16 * i if s == 2 else 0
            out = xc if s == 2 else dst
            for q in range(2):
                load_near(2 * i + q, s).wait()
            for q in range(2):
                for j in range(4):
                    low = lower_block(s, q, j)
                    high = low + (1 << s)
                    right = jnp.concatenate([src[low], src[high]], axis=0)
                    y = jnp.dot(ns[2 * i + q, 4 * s + j], right, preferred_element_type=jnp.float32)
                    y = y.astype(jnp.bfloat16)
                    out[base + low] = y[:PADR]
                    out[base + high] = y[PADR:]
            src, dst = dst, src
        return carry

    lax.fori_loop(0, 2, early, 0)

    def late(i, carry):
        for q in range(2):
            load_far(2 * i + q).wait()
        for q in range(2):
            for j in range(4):
                r, h = j // 2, j % 2
                low = 4 * i + 2 * q + r + 16 * h
                right = jnp.concatenate([xc[low], xc[low + 8]], axis=0)
                y = jnp.dot(fs[2 * i + q, j], right, preferred_element_type=jnp.float32).astype(jnp.bfloat16)
                xd[2 * q + r, 2 * h] = y[:PADR]
                xd[2 * q + r, 2 * h + 1] = y[PADR:]
        for q in range(2):
            for j in range(4):
                r, h = j // 2, j % 2
                right = jnp.concatenate([xd[2 * q + r, h], xd[2 * q + r, h + 2]], axis=0)
                y = jnp.dot(fs[2 * i + q, 4 + j], right, preferred_element_type=jnp.float32).astype(jnp.bfloat16)
                re = jnp.concatenate([y[:PADR, :HALF], y[PADR:, :HALF]], axis=1)
                im = jnp.concatenate([y[:PADR, HALF:], y[PADR:, HALF:]], axis=1)
                z = jnp.dot(order_ref[...], jnp.concatenate([re, im], axis=0), preferred_element_type=jnp.float32)
                for k in range(2):
                    for band in range(BANDS):
                        piece = z[band * SLOT:(band + 1) * SLOT, k * HALF:(k + 1) * HALF]
                        stage[h + 2 * k, 4 * i + 2 * q + r, band] = piece.astype(jnp.bfloat16)
            store(2 * i + q).start()
        return carry

    lax.fori_loop(0, 2, late, 0)
    for t in range(4):
        store(t).wait()


def butterfly(rx, first_row, near, far, rows):
    half = 0 if rows is None else 1
    anywhere = pl.BlockSpec(memory_space=pl.ANY)
    return pl.pallas_call(
        functools.partial(butterfly_kernel, half, first_row),
        out_shape=jax.ShapeDtypeStruct((4, 8, BANDS, SLOT, 2 * HALF), jnp.bfloat16),
        in_specs=[anywhere, anywhere, anywhere, pl.BlockSpec(memory_space=pltpu.VMEM)] + [anywhere] * half,
        out_specs=anywhere,
        scratch_shapes=[
            pltpu.VMEM((BLOCKS, XROWS, PART), jnp.bfloat16),
            pltpu.VMEM((4, 12, PAIR, PAIR), jnp.bfloat16),
            pltpu.VMEM((4, 8, PAIR, PAIR), jnp.bfloat16),
            pltpu.VMEM((4, 8, BANDS, SLOT, HALF), jnp.bfloat16),
            pltpu.VMEM((16, PADR, PART), jnp.bfloat16),
            pltpu.VMEM((16, PADR, PART), jnp.bfloat16),
            pltpu.VMEM((BLOCKS, PADR, PART), jnp.bfloat16),
            pltpu.VMEM((4, 4, PADR, PART), jnp.bfloat16),
            pltpu.SemaphoreType.DMA((4,)),
            pltpu.SemaphoreType.DMA((4, 3)),
            pltpu.SemaphoreType.DMA((4,)),
            pltpu.SemaphoreType.DMA((4,)),
        ],
        input_output_aliases={4: 0} if half else {},
        compiler_params=pltpu.CompilerParams(vmem_limit_bytes=56 << 20),
        name="butterfly",
    )(rx, near, far, send_order(), *([rows] * half))


def mirror_order():
    row = lax.broadcasted_iota(jnp.int32, (256, 256), 0)
    lane = lax.broadcasted_iota(jnp.int32, (256, 256), 1)
    return (row + lane == 256).astype(jnp.bfloat16)


def fourier_kernel(u_ref, order_ref, mirror_ref, table_ref, middle_ref, out_ref, v, vt, edge, buf, sem):
    step = pl.program_id(0)
    slot = step % 2
    tile = 256

    def copies(at, into):
        near = pltpu.make_async_copy(buf.at[into, 0], out_ref.at[:, :, pl.ds((4 - at) * tile, tile)], sem.at[into, 0])
        far = pltpu.make_async_copy(buf.at[into, 1], out_ref.at[:, :, pl.ds((5 + at) * tile, tile)], sem.at[into, 1])
        return near, far

    def sums(table):
        even = jnp.dot(vt[:, :640], table[:640], preferred_element_type=jnp.float32)
        odd = jnp.dot(vt[:, 640:], table[640:], preferred_element_type=jnp.float32)
        return even, odd

    @pl.when(step == 0)
    def _():
        for g in range(16):
            piece = u_ref[pl.ds(8 * g, 8)].reshape(8 * SLOT, PART)
            y = jnp.dot(order_ref[...], piece, preferred_element_type=jnp.float32)
            for p in range(2):
                for r in range(5):
                    at = p * 200 + r * 40
                    v[r, pl.ds(p * 640 + 40 * g, 40), :] = y[at:at + 40].astype(jnp.bfloat16)
        for r in range(5):
            vt[pl.ds(r * PART, PART), :] = v[r].T
        even, odd = sums(middle_ref[...])
        edge[...] = even - odd

    @pl.when(step >= 2)
    def _():
        for copy in copies(step - 2, slot):
            copy.wait()

    even, odd = sums(table_ref[...])
    near = (even + odd).astype(jnp.bfloat16)
    far = (even - odd).astype(jnp.bfloat16)
    turned = jnp.dot(far, mirror_ref[...], preferred_element_type=jnp.float32)
    lane = lax.broadcasted_iota(jnp.int32, (5 * PART, 128), 1)
    head = jnp.where(lane == 0, edge[...], turned[:, :128]).astype(jnp.bfloat16)
    tail = turned[:, 128:].astype(jnp.bfloat16)
    edge[...] = far[:, :128].astype(jnp.float32)
    for r in range(5):
        rows = slice(r * PART, (r + 1) * PART)
        buf[slot, 0, r] = near[rows]
        buf[slot, 1, r, :, pl.ds(0, 128)] = head[rows]
        buf[slot, 1, r, :, pl.ds(128, 128)] = tail[rows]
    for copy in copies(step, slot):
        copy.start()

    @pl.when(step == 4)
    def _():
        for copy in copies(3, 1) + copies(4, 0):
            copy.wait()


def fourier(u, table):
    return pl.pallas_call(
        fourier_kernel,
        out_shape=jax.ShapeDtypeStruct((5, PART, NLON), jnp.bfloat16),
        grid=(5,),
        in_specs=[
            pl.BlockSpec((BLOCKS * BANDS, SLOT, PART), lambda j: (0, 0, 0)),
            pl.BlockSpec((400, 8 * SLOT), lambda j: (0, 0)),
            pl.BlockSpec((256, 256), lambda j: (0, 0)),
            pl.BlockSpec((1280, 256), lambda j: (0, 4 - j)),
            pl.BlockSpec((1280, 128), lambda j: (0, 10)),
        ],
        out_specs=pl.BlockSpec(memory_space=pl.ANY),
        scratch_shapes=[
            pltpu.VMEM((5, 1280, PART), jnp.bfloat16),
            pltpu.VMEM((5 * PART, 1280), jnp.bfloat16),
            pltpu.VMEM((5 * PART, 128), jnp.float32),
            pltpu.VMEM((2, 2, 5, PART, 256), jnp.bfloat16),
            pltpu.SemaphoreType.DMA((2, 2)),
        ],
        compiler_params=pltpu.CompilerParams(vmem_limit_bytes=60 << 20),
        name="fourier",
    )(u, receive_order(), mirror_order(), table, table)


def fourier_table(ids):
    longitude = jnp.arange(NLON // 2 + 128, dtype=jnp.int32)
    phases = ids[:, None] * longitude[None, :] % NLON
    angles = phases.astype(jnp.float32) * (2.0 * math.pi / NLON)
    weight = jnp.where(ids == 0, 1.0, 2.0).astype(jnp.float32) / math.sqrt(2.0 * ids.shape[0])
    cosine_part = weight[:, None] * jnp.cos(angles)
    sine_part = -weight[:, None] * jnp.sin(angles)
    return jnp.concatenate([cosine_part, sine_part], axis=0).astype(jnp.bfloat16)


def body(coefficients, factors, wave_ids):
    wave_pos = lax.axis_index("wave")
    lev_pos = lax.axis_index("lev")
    rx0 = lax.all_to_all(pack_first(factors, coefficients), "wave", 0, 0, tiled=True)
    send1, rx0 = lax.optimization_barrier((pack_second(coefficients), rx0))
    rx1 = lax.all_to_all(send1, "wave", 0, 0, tiled=True)
    own_ids = lax.dynamic_slice_in_dim(wave_ids, lev_pos * (OWN * BLOCKS) + wave_pos * OWN, OWN, 0)
    first = (own_ids[:, None] - jnp.arange(DEG, dtype=jnp.int32)[None, :]).reshape(ROWS)
    first = jnp.pad(first, (0, PADR - ROWS))
    first = jnp.broadcast_to(jnp.concatenate([first, first])[None, :], (8, PAIR))
    near, far = section_factors(rx0, first)
    rows = butterfly(rx0, FROWS, near, far, None)
    rows, rx1 = lax.optimization_barrier((rows, rx1))
    rows = butterfly(rx1, 0, near, far, rows).reshape(BLOCKS * BANDS, SLOT, 2 * HALF)
    u = lax.all_to_all(rows, ("wave", "lev"), 0, 0, tiled=True)
    ids = wave_ids.reshape(BANDS, BLOCKS, OWN).transpose(1, 0, 2).reshape(-1)
    return fourier(u, fourier_table(ids))


def solution(mesh):
    in_specs = (P("wave", "lev", None), P(None, None, "wave", None, "lev"), P())
    out_specs = P(("wave", "lev"), None, None)
    return jax.shard_map(body, mesh=mesh, in_specs=in_specs, out_specs=out_specs, check_vma=False)
```

```python
import functools
import math

import jax
import jax.numpy as jnp
import numpy as np
from jax import lax
from jax.experimental import pallas as pl
from jax.experimental.pallas import tpu as pltpu
from jax.sharding import PartitionSpec as P

NLON = 2560
SECTIONS = 5
BLOCKS = 32
BANDS = 4
DEG = 20
OWN = 5
CH = 512
PART = 256
HALF = 128
ROWS = DEG * OWN
PADR = 112
SLOT = 56
PAIR = 2 * PADR
XROWS = 104
FROWS = 80


def select_matrices():
    shape = (SECTIONS, 2, 256, PAIR)
    s, v, q, lane = (lax.broadcasted_iota(jnp.int32, shape, d) for d in range(4))
    part = (lane // PADR) ^ v
    inner = lane % PADR
    hit = (q == s * 40 + (inner % DEG) * 2 + part) & (inner < ROWS)
    return hit.astype(jnp.bfloat16)


def diagonal_mask():
    row = lax.broadcasted_iota(jnp.int32, (PADR, PAIR), 0)
    inner = lax.broadcasted_iota(jnp.int32, (PADR, PAIR), 1) % PADR
    hit = (row // DEG == inner // DEG) & (row < ROWS) & (inner < ROWS)
    return hit.astype(jnp.float32)


def send_order():
    row = lax.broadcasted_iota(jnp.int32, (BANDS * SLOT, PAIR), 0)
    col = lax.broadcasted_iota(jnp.int32, (BANDS * SLOT, PAIR), 1)
    band, inner = row // SLOT, row % SLOT
    part, kr = inner // 25, inner % 25
    want = part * PADR + (kr // 5) * DEG + 5 * band + kr % 5
    return ((col == want) & (inner < 50)).astype(jnp.bfloat16)


def fill_pack_order(order):
    shape = (4 * 104, DEG * 24)
    row = lax.broadcasted_iota(jnp.int32, shape, 0)
    col = lax.broadcasted_iota(jnp.int32, shape, 1)
    owner = (row >= 104).astype(jnp.int32) + (row >= 208).astype(jnp.int32) + (row >= 312).astype(jnp.int32)
    inner = row - 104 * owner
    k = sum((inner >= DEG * i).astype(jnp.int32) for i in range(1, OWN))
    base = (inner - DEG * k) * 24 + OWN * owner + k
    ahead = jnp.where(inner < ROWS, col - base, -1)
    for v in range(2):
        order[v] = (ahead == 4 * v).astype(jnp.float32).astype(jnp.bfloat16)


def fold_lanes():
    f = np.zeros((256, 512), np.float32)
    for q in range(4):
        for j in range(50):
            f[50 * q + j, 128 * q + 72 + j] = 1
    return f


def fold_rows():
    f = np.zeros((FROWS, 96), np.float32)
    for q in range(4):
        for o in range(DEG):
            row = 16 * q + o if o < 16 else 64 + 4 * q + o - 16
            f[row, 24 * q + o] = 1
    return f


def chosen_rows(srcs, order, group):
    start = 4 * OWN * group
    at = start // 8 * 8
    window = jnp.concatenate([src[:, at:at + 24, :].reshape(DEG * 24, src.shape[2]) for src in srcs], axis=1)
    window = window.astype(jnp.bfloat16)
    return jnp.dot(order[(start - at) // 4], window, preferred_element_type=jnp.float32)


def pack_rows(srcs, order, out_ref, first):
    for group in range(BLOCKS // 4):
        y = chosen_rows(srcs, order, group)
        for d in range(4):
            out_ref[4 * group + d, pl.ds(first, XROWS), :] = y[XROWS * d:XROWS * (d + 1)].astype(jnp.bfloat16)


def pack_folded(src, order, lanes_ref, out_ref):
    for group in range(BLOCKS // 4):
        y = chosen_rows([src], order, group)
        rest = [y[XROWS * d + FROWS:XROWS * (d + 1)].astype(jnp.bfloat16) for d in range(4)]
        wide = jnp.dot(jnp.concatenate(rest, axis=0), lanes_ref[...], preferred_element_type=jnp.float32)
        for d in range(4):
            part = [wide[24 * d:24 * (d + 1), 128 * q:128 * (q + 1)] for q in range(4)]
            ends = [part[q][16:] + pltpu.roll(part[q + 1][16:], 4, 0) for q in (0, 2)]
            spare = jnp.concatenate([part[q][:16] for q in range(4)] + ends, axis=0)
            own = y[XROWS * d:XROWS * d + FROWS]
            out_ref[4 * group + d, pl.ds(0, FROWS), pl.ds(0, 128)] = own[:, :128].astype(jnp.bfloat16)
            out_ref[4 * group + d, pl.ds(0, FROWS), pl.ds(128, 128)] = (own[:, 128:] + spare).astype(jnp.bfloat16)


def pack_first_kernel(f_ref, eye_ref, lanes_ref, x_ref, out_ref, turned, order, xs, stage, sem, osem):
    fetch = [
        pltpu.make_async_copy(x_ref.at[:, :, pl.ds(p * PART, HALF)], xs.at[:, :, pl.ds(p * HALF, HALF)], sem.at[p])
        for p in range(2)
    ]
    for copy in fetch:
        copy.start()
    fill_pack_order(order)
    for o in range(DEG):
        left = jnp.concatenate([f_ref[s, o].reshape(2 * DEG, OWN * BLOCKS) for s in range(SECTIONS)], axis=0)
        y = lax.dot_general(left, eye_ref[...], (((0,), (0,)), ((), ())), preferred_element_type=jnp.float32)
        turned[o] = y
    pack_folded(turned, order, lanes_ref, stage)
    pieces = [pl.ds(0, FROWS), pl.ds(FROWS, XROWS)]
    store = [pltpu.make_async_copy(stage.at[:, at, :], out_ref.at[:, at, :], osem.at[i]) for i, at in enumerate(pieces)]
    store[0].start()
    for copy in fetch:
        copy.wait()
    for n in range(DEG):
        turned[n] = xs[n].astype(jnp.float32)
    pack_rows([turned], order, stage, FROWS)
    store[1].start()
    for copy in store:
        copy.wait()


def pack_first(factors, x):
    here = pl.BlockSpec(memory_space=pltpu.VMEM)
    return pl.pallas_call(
        pack_first_kernel,
        out_shape=jax.ShapeDtypeStruct((BLOCKS, FROWS + XROWS, PART), jnp.bfloat16),
        in_specs=[here, here, here, pl.BlockSpec(memory_space=pl.ANY)],
        out_specs=pl.BlockSpec(memory_space=pl.ANY),
        scratch_shapes=[
            pltpu.VMEM((DEG, OWN * BLOCKS, 256), jnp.float32),
            pltpu.VMEM((2, 416, 480), jnp.bfloat16),
            pltpu.VMEM((DEG, OWN * BLOCKS, PART), jnp.bfloat16),
            pltpu.VMEM((BLOCKS, FROWS + XROWS, PART), jnp.bfloat16),
            pltpu.SemaphoreType.DMA((2,)),
            pltpu.SemaphoreType.DMA((2,)),
        ],
        compiler_params=pltpu.CompilerParams(vmem_limit_bytes=60 << 20),
        name="pack_first",
    )(
        factors.transpose(0, 2, 3, 1, 4),
        jnp.asarray(np.eye(200, 256), jnp.bfloat16),
        jnp.asarray(fold_lanes(), jnp.bfloat16),
        x,
    )


def pack_second_kernel(re_ref, im_ref, out_ref, order, wide):
    fill_pack_order(order)
    for n in range(DEG):
        wide[n, :, pl.ds(0, HALF)] = re_ref[n].astype(jnp.float32)
        wide[n, :, pl.ds(HALF, HALF)] = im_ref[n].astype(jnp.float32)
    pack_rows([wide], order, out_ref, 0)


def pack_second(x):
    return pl.pallas_call(
        pack_second_kernel,
        out_shape=jax.ShapeDtypeStruct((BLOCKS, XROWS, PART), jnp.bfloat16),
        grid=(1,),
        in_specs=[
            pl.BlockSpec((DEG, OWN * BLOCKS, HALF), lambda i: (0, 0, 1)),
            pl.BlockSpec((DEG, OWN * BLOCKS, HALF), lambda i: (0, 0, 3)),
        ],
        out_specs=pl.BlockSpec((BLOCKS, XROWS, PART), lambda i: (0, 0, 0)),
        scratch_shapes=[pltpu.VMEM((2, 416, 480), jnp.bfloat16), pltpu.VMEM((DEG, OWN * BLOCKS, PART), jnp.float32)],
        compiler_params=pltpu.CompilerParams(vmem_limit_bytes=60 << 20),
        name="pack_second",
    )(x, x)


def receive_order():
    row = lax.broadcasted_iota(jnp.int32, (400, 8 * SLOT), 0)
    col = lax.broadcasted_iota(jnp.int32, (400, 8 * SLOT), 1)
    part, lat = row // 200, (row // 40) % 5
    src, k = (row % 40) // 5, row % 5
    return (col == src * SLOT + part * 25 + k * 5 + lat).astype(jnp.bfloat16)


def lower_block(s, group, j):
    if s < 3:
        return 8 * group + (j >> s) * (2 << s) + (j & ((1 << s) - 1))
    step = 16 if s == 3 else 8
    return 2 * group + j // 2 + step * (j % 2)


def section_kernel(rf_ref, e_ref, mask_ref, first_ref, lanes_ref, rows_ref, near_ref, far_ref, fc):
    zeros_f = jnp.zeros((16, 256), jnp.bfloat16)
    rest = []
    for b in range(BLOCKS):
        fc[b, pl.ds(96, 16), :] = zeros_f
        fc[b, pl.ds(0, FROWS), :] = rf_ref[b]
        tall = jnp.dot(rows_ref[...], rf_ref[b, :, 128:], preferred_element_type=jnp.float32)
        rest.append(jnp.concatenate([tall[24 * q:24 * (q + 1)] for q in range(4)], axis=1))
    rest = jnp.concatenate(rest, axis=0).astype(jnp.bfloat16)
    rest = jnp.dot(rest, lanes_ref[...], preferred_element_type=jnp.float32)
    for b in range(BLOCKS):
        fc[b, pl.ds(FROWS, 24), :] = rest[24 * b:24 * (b + 1)].astype(jnp.bfloat16)
    lane_high = lax.broadcasted_iota(jnp.int32, (8, PAIR), 1) // PADR
    mask = mask_ref[...]
    for s in range(SECTIONS):
        lows = [(g, j, lower_block(s, g, j)) for g in range(4) for j in range(4)]
        for v in range(2):
            left = jnp.concatenate([fc[low + (v << s)] for _, _, low in lows], axis=0)
            f = jnp.dot(left, e_ref[s, v], preferred_element_type=jnp.float32)
            for i, (g, j, low) in enumerate(lows):
                keep = mask
                if s == 0:
                    start = DEG * (low + lane_high)
                    live = (start >= first_ref[...]).astype(jnp.float32)
                    keep = mask * live[0:1, :]
                piece = (f[i * PADR:(i + 1) * PADR] * keep).astype(jnp.bfloat16)
                if s < 3:
                    near_ref[g, 4 * s + j, pl.ds(v * PADR, PADR), :] = piece
                else:
                    far_ref[g, 4 * (s - 3) + j, pl.ds(v * PADR, PADR), :] = piece


def section_factors(rf, first):
    return pl.pallas_call(
        section_kernel,
        out_shape=[
            jax.ShapeDtypeStruct((4, 12, PAIR, PAIR), jnp.bfloat16),
            jax.ShapeDtypeStruct((4, 8, PAIR, PAIR), jnp.bfloat16),
        ],
        grid=(1,),
        in_specs=[
            pl.BlockSpec((BLOCKS, FROWS, 256), lambda i: (0, 0, 0)),
            pl.BlockSpec((SECTIONS, 2, 256, PAIR), lambda i: (0, 0, 0, 0)),
            pl.BlockSpec((PADR, PAIR), lambda i: (0, 0)),
            pl.BlockSpec((8, PAIR), lambda i: (0, 0)),
            pl.BlockSpec((512, 256), lambda i: (0, 0)),
            pl.BlockSpec((96, FROWS), lambda i: (0, 0)),
        ],
        out_specs=[
            pl.BlockSpec((4, 12, PAIR, PAIR), lambda i: (0, 0, 0, 0)),
            pl.BlockSpec((4, 8, PAIR, PAIR), lambda i: (0, 0, 0, 0)),
        ],
        scratch_shapes=[pltpu.VMEM((BLOCKS, PADR, 256), jnp.bfloat16)],
        compiler_params=pltpu.CompilerParams(vmem_limit_bytes=58 << 20),
        name="section_factors",
    )(
        rf, select_matrices(), diagonal_mask(), first,
        jnp.asarray(fold_lanes().T, jnp.bfloat16), jnp.asarray(fold_rows().T, jnp.bfloat16),
    )


def butterfly_kernel(half, first_row, rx_ref, near_ref, far_ref, order_ref, *refs):
    out_ref, rs, ns, fs, stage, xa, xb, xc, xd, rsem, nsem, fsem, osem = refs[-13:]

    def load_rows(g):
        rows = rx_ref.at[pl.ds(8 * g, 8), pl.ds(first_row, XROWS), :]
        return pltpu.make_async_copy(rows, rs.at[pl.ds(8 * g, 8)], rsem.at[g])

    def load_near(g, s):
        return pltpu.make_async_copy(near_ref.at[g, pl.ds(4 * s, 4)], ns.at[g, pl.ds(4 * s, 4)], nsem.at[g, s])

    def load_far(t):
        return pltpu.make_async_copy(far_ref.at[t], fs.at[t], fsem.at[t])

    def store(t):
        rows = out_ref.at[:, pl.ds(2 * t, 2), :, :, pl.ds(HALF * half, HALF)]
        return pltpu.make_async_copy(stage.at[:, pl.ds(2 * t, 2)], rows, osem.at[t])

    for g in range(4):
        load_rows(g).start()
        for s in range(3):
            load_near(g, s).start()
    for t in range(4):
        load_far(t).start()
    for b in range(16):
        xa[b, pl.ds(96, 16), :] = jnp.zeros((16, PART), jnp.bfloat16)

    def early(i, carry):
        for q in range(2):
            load_rows(2 * i + q).wait()
            for b in range(8):
                xa[8 * q + b, pl.ds(0, XROWS), :] = rs[16 * i + 8 * q + b]
        src, dst = xa, xb
        for s in range(3):
            base = 16 * i if s == 2 else 0
            out = xc if s == 2 else dst
            for q in range(2):
                load_near(2 * i + q, s).wait()
            for q in range(2):
                for j in range(4):
                    low = lower_block(s, q, j)
                    high = low + (1 << s)
                    right = jnp.concatenate([src[low], src[high]], axis=0)
                    y = jnp.dot(ns[2 * i + q, 4 * s + j], right, preferred_element_type=jnp.float32)
                    y = y.astype(jnp.bfloat16)
                    out[base + low] = y[:PADR]
                    out[base + high] = y[PADR:]
            src, dst = dst, src
        return carry

    lax.fori_loop(0, 2, early, 0)

    def late(i, carry):
        for q in range(2):
            load_far(2 * i + q).wait()
        for q in range(2):
            for j in range(4):
                r, h = j // 2, j % 2
                low = 4 * i + 2 * q + r + 16 * h
                right = jnp.concatenate([xc[low], xc[low + 8]], axis=0)
                y = jnp.dot(fs[2 * i + q, j], right, preferred_element_type=jnp.float32).astype(jnp.bfloat16)
                xd[2 * q + r, 2 * h] = y[:PADR]
                xd[2 * q + r, 2 * h + 1] = y[PADR:]
        for q in range(2):
            for j in range(4):
                r, h = j // 2, j % 2
                right = jnp.concatenate([xd[2 * q + r, h], xd[2 * q + r, h + 2]], axis=0)
                y = jnp.dot(fs[2 * i + q, 4 + j], right, preferred_element_type=jnp.float32).astype(jnp.bfloat16)
                re = jnp.concatenate([y[:PADR, :HALF], y[PADR:, :HALF]], axis=1)
                im = jnp.concatenate([y[:PADR, HALF:], y[PADR:, HALF:]], axis=1)
                z = jnp.dot(order_ref[...], jnp.concatenate([re, im], axis=0), preferred_element_type=jnp.float32)
                for k in range(2):
                    for band in range(BANDS):
                        piece = z[band * SLOT:(band + 1) * SLOT, k * HALF:(k + 1) * HALF]
                        stage[h + 2 * k, 4 * i + 2 * q + r, band] = piece.astype(jnp.bfloat16)
            store(2 * i + q).start()
        return carry

    lax.fori_loop(0, 2, late, 0)
    for t in range(4):
        store(t).wait()


def butterfly(rx, first_row, near, far, rows):
    half = 0 if rows is None else 1
    anywhere = pl.BlockSpec(memory_space=pl.ANY)
    return pl.pallas_call(
        functools.partial(butterfly_kernel, half, first_row),
        out_shape=jax.ShapeDtypeStruct((4, 8, BANDS, SLOT, 2 * HALF), jnp.bfloat16),
        in_specs=[anywhere, anywhere, anywhere, pl.BlockSpec(memory_space=pltpu.VMEM)] + [anywhere] * half,
        out_specs=anywhere,
        scratch_shapes=[
            pltpu.VMEM((BLOCKS, XROWS, PART), jnp.bfloat16),
            pltpu.VMEM((4, 12, PAIR, PAIR), jnp.bfloat16),
            pltpu.VMEM((4, 8, PAIR, PAIR), jnp.bfloat16),
            pltpu.VMEM((4, 8, BANDS, SLOT, HALF), jnp.bfloat16),
            pltpu.VMEM((16, PADR, PART), jnp.bfloat16),
            pltpu.VMEM((16, PADR, PART), jnp.bfloat16),
            pltpu.VMEM((BLOCKS, PADR, PART), jnp.bfloat16),
            pltpu.VMEM((4, 4, PADR, PART), jnp.bfloat16),
            pltpu.SemaphoreType.DMA((4,)),
            pltpu.SemaphoreType.DMA((4, 3)),
            pltpu.SemaphoreType.DMA((4,)),
            pltpu.SemaphoreType.DMA((4,)),
        ],
        input_output_aliases={4: 0} if half else {},
        compiler_params=pltpu.CompilerParams(vmem_limit_bytes=56 << 20),
        name="butterfly",
    )(rx, near, far, send_order(), *([rows] * half))


def mirror_order():
    row = lax.broadcasted_iota(jnp.int32, (256, 256), 0)
    lane = lax.broadcasted_iota(jnp.int32, (256, 256), 1)
    return (row + lane == 256).astype(jnp.bfloat16)


def fourier_kernel(u_ref, order_ref, mirror_ref, table_ref, middle_ref, out_ref, v, vt, edge, buf, sem):
    step = pl.program_id(0)
    slot = step % 2
    tile = 256

    def copies(at, into):
        near = pltpu.make_async_copy(buf.at[into, 0], out_ref.at[:, :, pl.ds((4 - at) * tile, tile)], sem.at[into, 0])
        far = pltpu.make_async_copy(buf.at[into, 1], out_ref.at[:, :, pl.ds((5 + at) * tile, tile)], sem.at[into, 1])
        return near, far

    def sums(table):
        even = jnp.dot(vt[:, :640], table[:640], preferred_element_type=jnp.float32)
        odd = jnp.dot(vt[:, 640:], table[640:], preferred_element_type=jnp.float32)
        return even, odd

    @pl.when(step == 0)
    def _():
        for g in range(16):
            piece = u_ref[pl.ds(8 * g, 8)].reshape(8 * SLOT, PART)
            y = jnp.dot(order_ref[...], piece, preferred_element_type=jnp.float32)
            for p in range(2):
                for r in range(5):
                    at = p * 200 + r * 40
                    v[r, pl.ds(p * 640 + 40 * g, 40), :] = y[at:at + 40].astype(jnp.bfloat16)
        for r in range(5):
            vt[pl.ds(r * PART, PART), :] = v[r].T
        even, odd = sums(middle_ref[...])
        edge[...] = even - odd

    @pl.when(step >= 2)
    def _():
        for copy in copies(step - 2, slot):
            copy.wait()

    even, odd = sums(table_ref[...])
    near = (even + odd).astype(jnp.bfloat16)
    far = (even - odd).astype(jnp.bfloat16)
    turned = jnp.dot(far, mirror_ref[...], preferred_element_type=jnp.float32)
    lane = lax.broadcasted_iota(jnp.int32, (5 * PART, 128), 1)
    head = jnp.where(lane == 0, edge[...], turned[:, :128]).astype(jnp.bfloat16)
    tail = turned[:, 128:].astype(jnp.bfloat16)
    edge[...] = far[:, :128].astype(jnp.float32)
    for r in range(5):
        rows = slice(r * PART, (r + 1) * PART)
        buf[slot, 0, r] = near[rows]
        buf[slot, 1, r, :, pl.ds(0, 128)] = head[rows]
        buf[slot, 1, r, :, pl.ds(128, 128)] = tail[rows]
    for copy in copies(step, slot):
        copy.start()

    @pl.when(step == 4)
    def _():
        for copy in copies(3, 1) + copies(4, 0):
            copy.wait()


def fourier(u, table):
    return pl.pallas_call(
        fourier_kernel,
        out_shape=jax.ShapeDtypeStruct((5, PART, NLON), jnp.bfloat16),
        grid=(5,),
        in_specs=[
            pl.BlockSpec((BLOCKS * BANDS, SLOT, PART), lambda j: (0, 0, 0)),
            pl.BlockSpec((400, 8 * SLOT), lambda j: (0, 0)),
            pl.BlockSpec((256, 256), lambda j: (0, 0)),
            pl.BlockSpec((1280, 256), lambda j: (0, 4 - j)),
            pl.BlockSpec((1280, 128), lambda j: (0, 10)),
        ],
        out_specs=pl.BlockSpec(memory_space=pl.ANY),
        scratch_shapes=[
            pltpu.VMEM((5, 1280, PART), jnp.bfloat16),
            pltpu.VMEM((5 * PART, 1280), jnp.bfloat16),
            pltpu.VMEM((5 * PART, 128), jnp.float32),
            pltpu.VMEM((2, 2, 5, PART, 256), jnp.bfloat16),
            pltpu.SemaphoreType.DMA((2, 2)),
        ],
        compiler_params=pltpu.CompilerParams(vmem_limit_bytes=60 << 20),
        name="fourier",
    )(u, receive_order(), mirror_order(), table, table)


def fourier_table(ids):
    longitude = jnp.arange(NLON // 2 + 128, dtype=jnp.int32)
    phases = ids[:, None] * longitude[None, :] % NLON
    angles = phases.astype(jnp.float32) * (2.0 * math.pi / NLON)
    weight = jnp.where(ids == 0, 1.0, 2.0).astype(jnp.float32) / math.sqrt(2.0 * ids.shape[0])
    cosine_part = weight[:, None] * jnp.cos(angles)
    sine_part = -weight[:, None] * jnp.sin(angles)
    return jnp.concatenate([cosine_part, sine_part], axis=0).astype(jnp.bfloat16)


def body(coefficients, factors, wave_ids):
    wave_pos = lax.axis_index("wave")
    lev_pos = lax.axis_index("lev")
    rx0 = lax.all_to_all(pack_first(factors, coefficients), "wave", 0, 0, tiled=True)
    send1, rx0 = lax.optimization_barrier((pack_second(coefficients), rx0))
    rx1 = lax.all_to_all(send1, "wave", 0, 0, tiled=True)
    own_ids = lax.dynamic_slice_in_dim(wave_ids, lev_pos * (OWN * BLOCKS) + wave_pos * OWN, OWN, 0)
    first = (own_ids[:, None] - jnp.arange(DEG, dtype=jnp.int32)[None, :]).reshape(ROWS)
    first = jnp.pad(first, (0, PADR - ROWS))
    first = jnp.broadcast_to(jnp.concatenate([first, first])[None, :], (8, PAIR))
    near, far = section_factors(rx0, first)
    rows = butterfly(rx0, FROWS, near, far, None)
    rows, rx1 = lax.optimization_barrier((rows, rx1))
    rows = butterfly(rx1, 0, near, far, rows).reshape(BLOCKS * BANDS, SLOT, 2 * HALF)
    u = lax.all_to_all(rows, ("wave", "lev"), 0, 0, tiled=True)
    ids = wave_ids.reshape(BANDS, BLOCKS, OWN).transpose(1, 0, 2).reshape(-1)
    return fourier(u, fourier_table(ids))


def solution(mesh):
    in_specs = (P("wave", "lev", None), P(None, None, "wave", None, "lev"), P())
    out_specs = P(("wave", "lev"), None, None)
    return jax.shard_map(body, mesh=mesh, in_specs=in_specs, out_specs=out_specs, check_vma=False)
```

```python
import functools
import math

import jax
import jax.numpy as jnp
import numpy as np
from jax import lax
from jax.experimental import pallas as pl
from jax.experimental.pallas import tpu as pltpu
from jax.sharding import PartitionSpec as P

NLON = 2560
SECTIONS = 5
BLOCKS = 32
BANDS = 4
DEG = 20
OWN = 5
CH = 512
PART = 256
HALF = 128
ROWS = DEG * OWN
PADR = 112
SLOT = 56
PAIR = 2 * PADR
XROWS = 104
FROWS = 80


def select_matrices():
    shape = (SECTIONS, 2, 256, PAIR)
    s, v, q, lane = (lax.broadcasted_iota(jnp.int32, shape, d) for d in range(4))
    part = (lane // PADR) ^ v
    inner = lane % PADR
    hit = (q == s * 40 + (inner % DEG) * 2 + part) & (inner < ROWS)
    return hit.astype(jnp.bfloat16)


def diagonal_mask():
    row = lax.broadcasted_iota(jnp.int32, (PADR, PAIR), 0)
    inner = lax.broadcasted_iota(jnp.int32, (PADR, PAIR), 1) % PADR
    hit = (row // DEG == inner // DEG) & (row < ROWS) & (inner < ROWS)
    return hit.astype(jnp.float32)


def send_order():
    row = lax.broadcasted_iota(jnp.int32, (BANDS * SLOT, PAIR), 0)
    col = lax.broadcasted_iota(jnp.int32, (BANDS * SLOT, PAIR), 1)
    band, inner = row // SLOT, row % SLOT
    part, kr = inner // 25, inner % 25
    want = part * PADR + (kr // 5) * DEG + 5 * band + kr % 5
    return ((col == want) & (inner < 50)).astype(jnp.bfloat16)


def fill_pack_order(order):
    shape = (4 * 104, DEG * 24)
    row = lax.broadcasted_iota(jnp.int32, shape, 0)
    col = lax.broadcasted_iota(jnp.int32, shape, 1)
    owner = (row >= 104).astype(jnp.int32) + (row >= 208).astype(jnp.int32) + (row >= 312).astype(jnp.int32)
    inner = row - 104 * owner
    k = sum((inner >= DEG * i).astype(jnp.int32) for i in range(1, OWN))
    base = (inner - DEG * k) * 24 + OWN * owner + k
    ahead = jnp.where(inner < ROWS, col - base, -1)
    for v in range(2):
        order[v] = (ahead == 4 * v).astype(jnp.float32).astype(jnp.bfloat16)


def fold_lanes():
    f = np.zeros((256, 512), np.float32)
    for q in range(4):
        for j in range(50):
            f[50 * q + j, 128 * q + 72 + j] = 1
    return f


def fold_rows():
    f = np.zeros((FROWS, 96), np.float32)
    for q in range(4):
        for o in range(DEG):
            row = 16 * q + o if o < 16 else 64 + 4 * q + o - 16
            f[row, 24 * q + o] = 1
    return f


def chosen_rows(srcs, order, group):
    start = 4 * OWN * group
    at = start // 8 * 8
    window = jnp.concatenate([src[:, at:at + 24, :].reshape(DEG * 24, src.shape[2]) for src in srcs], axis=1)
    window = window.astype(jnp.bfloat16)
    return jnp.dot(order[(start - at) // 4], window, preferred_element_type=jnp.float32)


def pack_rows(srcs, order, out_ref, first):
    for group in range(BLOCKS // 4):
        y = chosen_rows(srcs, order, group)
        for d in range(4):
            out_ref[4 * group + d, pl.ds(first, XROWS), :] = y[XROWS * d:XROWS * (d + 1)].astype(jnp.bfloat16)


def pack_folded(src, order, lanes_ref, out_ref):
    for group in range(BLOCKS // 4):
        y = chosen_rows([src], order, group)
        rest = [y[XROWS * d + FROWS:XROWS * (d + 1)].astype(jnp.bfloat16) for d in range(4)]
        wide = jnp.dot(jnp.concatenate(rest, axis=0), lanes_ref[...], preferred_element_type=jnp.float32)
        for d in range(4):
            part = [wide[24 * d:24 * (d + 1), 128 * q:128 * (q + 1)] for q in range(4)]
            ends = [part[q][16:] + pltpu.roll(part[q + 1][16:], 4, 0) for q in (0, 2)]
            spare = jnp.concatenate([part[q][:16] for q in range(4)] + ends, axis=0)
            own = y[XROWS * d:XROWS * d + FROWS]
            out_ref[4 * group + d, pl.ds(0, FROWS), pl.ds(0, 128)] = own[:, :128].astype(jnp.bfloat16)
            out_ref[4 * group + d, pl.ds(0, FROWS), pl.ds(128, 128)] = (own[:, 128:] + spare).astype(jnp.bfloat16)


def pack_first_kernel(f_ref, eye_ref, lanes_ref, x_ref, out_ref, turned, order, xs, stage, sem, osem):
    fetch = [
        pltpu.make_async_copy(x_ref.at[:, :, pl.ds(p * PART, HALF)], xs.at[:, :, pl.ds(p * HALF, HALF)], sem.at[p])
        for p in range(2)
    ]
    for copy in fetch:
        copy.start()
    fill_pack_order(order)
    for o in range(DEG):
        left = jnp.concatenate([f_ref[s, o].reshape(2 * DEG, OWN * BLOCKS) for s in range(SECTIONS)], axis=0)
        y = lax.dot_general(left, eye_ref[...], (((0,), (0,)), ((), ())), preferred_element_type=jnp.float32)
        turned[o] = y
    pack_folded(turned, order, lanes_ref, stage)
    pieces = [pl.ds(0, FROWS), pl.ds(FROWS, XROWS)]
    store = [pltpu.make_async_copy(stage.at[:, at, :], out_ref.at[:, at, :], osem.at[i]) for i, at in enumerate(pieces)]
    store[0].start()
    for copy in fetch:
        copy.wait()
    for n in range(DEG):
        turned[n] = xs[n].astype(jnp.float32)
    pack_rows([turned], order, stage, FROWS)
    store[1].start()
    for copy in store:
        copy.wait()


def pack_first(factors, x):
    here = pl.BlockSpec(memory_space=pltpu.VMEM)
    return pl.pallas_call(
        pack_first_kernel,
        out_shape=jax.ShapeDtypeStruct((BLOCKS, FROWS + XROWS, PART), jnp.bfloat16),
        in_specs=[here, here, here, pl.BlockSpec(memory_space=pl.ANY)],
        out_specs=pl.BlockSpec(memory_space=pl.ANY),
        scratch_shapes=[
            pltpu.VMEM((DEG, OWN * BLOCKS, 256), jnp.float32),
            pltpu.VMEM((2, 416, 480), jnp.bfloat16),
            pltpu.VMEM((DEG, OWN * BLOCKS, PART), jnp.bfloat16),
            pltpu.VMEM((BLOCKS, FROWS + XROWS, PART), jnp.bfloat16),
            pltpu.SemaphoreType.DMA((2,)),
            pltpu.SemaphoreType.DMA((2,)),
        ],
        compiler_params=pltpu.CompilerParams(vmem_limit_bytes=60 << 20),
        name="pack_first",
    )(
        factors.transpose(0, 2, 3, 1, 4),
        jnp.asarray(np.eye(200, 256), jnp.bfloat16),
        jnp.asarray(fold_lanes(), jnp.bfloat16),
        x,
    )


def pack_second_kernel(re_ref, im_ref, out_ref, order, wide):
    fill_pack_order(order)
    for n in range(DEG):
        wide[n, :, pl.ds(0, HALF)] = re_ref[n].astype(jnp.float32)
        wide[n, :, pl.ds(HALF, HALF)] = im_ref[n].astype(jnp.float32)
    pack_rows([wide], order, out_ref, 0)


def pack_second(x):
    return pl.pallas_call(
        pack_second_kernel,
        out_shape=jax.ShapeDtypeStruct((BLOCKS, XROWS, PART), jnp.bfloat16),
        grid=(1,),
        in_specs=[
            pl.BlockSpec((DEG, OWN * BLOCKS, HALF), lambda i: (0, 0, 1)),
            pl.BlockSpec((DEG, OWN * BLOCKS, HALF), lambda i: (0, 0, 3)),
        ],
        out_specs=pl.BlockSpec((BLOCKS, XROWS, PART), lambda i: (0, 0, 0)),
        scratch_shapes=[pltpu.VMEM((2, 416, 480), jnp.bfloat16), pltpu.VMEM((DEG, OWN * BLOCKS, PART), jnp.float32)],
        compiler_params=pltpu.CompilerParams(vmem_limit_bytes=60 << 20),
        name="pack_second",
    )(x, x)


def receive_order():
    row = lax.broadcasted_iota(jnp.int32, (400, 8 * SLOT), 0)
    col = lax.broadcasted_iota(jnp.int32, (400, 8 * SLOT), 1)
    part, lat = row // 200, (row // 40) % 5
    src, k = (row % 40) // 5, row % 5
    return (col == src * SLOT + part * 25 + k * 5 + lat).astype(jnp.bfloat16)


def lower_block(s, group, j):
    if s < 3:
        return 8 * group + (j >> s) * (2 << s) + (j & ((1 << s) - 1))
    step = 16 if s == 3 else 8
    return 2 * group + j // 2 + step * (j % 2)


def section_kernel(rf_ref, e_ref, mask_ref, first_ref, lanes_ref, rows_ref, near_ref, far_ref, fc):
    zeros_f = jnp.zeros((16, 256), jnp.bfloat16)
    rest = []
    for b in range(BLOCKS):
        fc[b, pl.ds(96, 16), :] = zeros_f
        fc[b, pl.ds(0, FROWS), :] = rf_ref[b]
        tall = jnp.dot(rows_ref[...], rf_ref[b, :, 128:], preferred_element_type=jnp.float32)
        rest.append(jnp.concatenate([tall[24 * q:24 * (q + 1)] for q in range(4)], axis=1))
    rest = jnp.concatenate(rest, axis=0).astype(jnp.bfloat16)
    rest = jnp.dot(rest, lanes_ref[...], preferred_element_type=jnp.float32)
    for b in range(BLOCKS):
        fc[b, pl.ds(FROWS, 24), :] = rest[24 * b:24 * (b + 1)].astype(jnp.bfloat16)
    lane_high = lax.broadcasted_iota(jnp.int32, (8, PAIR), 1) // PADR
    mask = mask_ref[...]
    for s in range(SECTIONS):
        lows = [(g, j, lower_block(s, g, j)) for g in range(4) for j in range(4)]
        for v in range(2):
            left = jnp.concatenate([fc[low + (v << s)] for _, _, low in lows], axis=0)
            f = jnp.dot(left, e_ref[s, v], preferred_element_type=jnp.float32)
            for i, (g, j, low) in enumerate(lows):
                keep = mask
                if s == 0:
                    start = DEG * (low + lane_high)
                    live = (start >= first_ref[...]).astype(jnp.float32)
                    keep = mask * live[0:1, :]
                piece = (f[i * PADR:(i + 1) * PADR] * keep).astype(jnp.bfloat16)
                if s < 3:
                    near_ref[g, 4 * s + j, pl.ds(v * PADR, PADR), :] = piece
                else:
                    far_ref[g, 4 * (s - 3) + j, pl.ds(v * PADR, PADR), :] = piece


def section_factors(rf, first):
    return pl.pallas_call(
        section_kernel,
        out_shape=[
            jax.ShapeDtypeStruct((4, 12, PAIR, PAIR), jnp.bfloat16),
            jax.ShapeDtypeStruct((4, 8, PAIR, PAIR), jnp.bfloat16),
        ],
        grid=(1,),
        in_specs=[
            pl.BlockSpec((BLOCKS, FROWS, 256), lambda i: (0, 0, 0)),
            pl.BlockSpec((SECTIONS, 2, 256, PAIR), lambda i: (0, 0, 0, 0)),
            pl.BlockSpec((PADR, PAIR), lambda i: (0, 0)),
            pl.BlockSpec((8, PAIR), lambda i: (0, 0)),
            pl.BlockSpec((512, 256), lambda i: (0, 0)),
            pl.BlockSpec((96, FROWS), lambda i: (0, 0)),
        ],
        out_specs=[
            pl.BlockSpec((4, 12, PAIR, PAIR), lambda i: (0, 0, 0, 0)),
            pl.BlockSpec((4, 8, PAIR, PAIR), lambda i: (0, 0, 0, 0)),
        ],
        scratch_shapes=[pltpu.VMEM((BLOCKS, PADR, 256), jnp.bfloat16)],
        compiler_params=pltpu.CompilerParams(vmem_limit_bytes=58 << 20),
        name="section_factors",
    )(
        rf, select_matrices(), diagonal_mask(), first,
        jnp.asarray(fold_lanes().T, jnp.bfloat16), jnp.asarray(fold_rows().T, jnp.bfloat16),
    )


def butterfly_kernel(half, first_row, rx_ref, near_ref, far_ref, order_ref, *refs):
    out_ref, rs, ns, fs, stage, xa, xb, xc, xd, rsem, nsem, fsem, osem = refs[-13:]

    def load_rows(g):
        rows = rx_ref.at[pl.ds(8 * g, 8), pl.ds(first_row, XROWS), :]
        return pltpu.make_async_copy(rows, rs.at[pl.ds(8 * g, 8)], rsem.at[g])

    def load_near(g, s):
        return pltpu.make_async_copy(near_ref.at[g, pl.ds(4 * s, 4)], ns.at[g, pl.ds(4 * s, 4)], nsem.at[g, s])

    def load_far(t):
        return pltpu.make_async_copy(far_ref.at[t], fs.at[t], fsem.at[t])

    def store(t):
        rows = out_ref.at[:, pl.ds(2 * t, 2), :, :, pl.ds(HALF * half, HALF)]
        return pltpu.make_async_copy(stage.at[:, pl.ds(2 * t, 2)], rows, osem.at[t])

    for g in range(4):
        load_rows(g).start()
        for s in range(3):
            load_near(g, s).start()
    for t in range(4):
        load_far(t).start()
    for b in range(16):
        xa[b, pl.ds(96, 16), :] = jnp.zeros((16, PART), jnp.bfloat16)

    def early(i, carry):
        for q in range(2):
            load_rows(2 * i + q).wait()
            for b in range(8):
                xa[8 * q + b, pl.ds(0, XROWS), :] = rs[16 * i + 8 * q + b]
        src, dst = xa, xb
        for s in range(3):
            base = 16 * i if s == 2 else 0
            out = xc if s == 2 else dst
            for q in range(2):
                load_near(2 * i + q, s).wait()
            for q in range(2):
                for j in range(4):
                    low = lower_block(s, q, j)
                    high = low + (1 << s)
                    right = jnp.concatenate([src[low], src[high]], axis=0)
                    y = jnp.dot(ns[2 * i + q, 4 * s + j], right, preferred_element_type=jnp.float32)
                    y = y.astype(jnp.bfloat16)
                    out[base + low] = y[:PADR]
                    out[base + high] = y[PADR:]
            src, dst = dst, src
        return carry

    lax.fori_loop(0, 2, early, 0, unroll=True)

    def late(i, carry):
        for q in range(2):
            load_far(2 * i + q).wait()
        for q in range(2):
            for j in range(4):
                r, h = j // 2, j % 2
                low = 4 * i + 2 * q + r + 16 * h
                right = jnp.concatenate([xc[low], xc[low + 8]], axis=0)
                y = jnp.dot(fs[2 * i + q, j], right, preferred_element_type=jnp.float32).astype(jnp.bfloat16)
                xd[2 * q + r, 2 * h] = y[:PADR]
                xd[2 * q + r, 2 * h + 1] = y[PADR:]
        for q in range(2):
            for j in range(4):
                r, h = j // 2, j % 2
                right = jnp.concatenate([xd[2 * q + r, h], xd[2 * q + r, h + 2]], axis=0)
                y = jnp.dot(fs[2 * i + q, 4 + j], right, preferred_element_type=jnp.float32).astype(jnp.bfloat16)
                re = jnp.concatenate([y[:PADR, :HALF], y[PADR:, :HALF]], axis=1)
                im = jnp.concatenate([y[:PADR, HALF:], y[PADR:, HALF:]], axis=1)
                z = jnp.dot(order_ref[...], jnp.concatenate([re, im], axis=0), preferred_element_type=jnp.float32)
                for k in range(2):
                    for band in range(BANDS):
                        piece = z[band * SLOT:(band + 1) * SLOT, k * HALF:(k + 1) * HALF]
                        stage[h + 2 * k, 4 * i + 2 * q + r, band] = piece.astype(jnp.bfloat16)
            store(2 * i + q).start()
        return carry

    lax.fori_loop(0, 2, late, 0, unroll=True)
    for t in range(4):
        store(t).wait()


def butterfly(rx, first_row, near, far, rows):
    half = 0 if rows is None else 1
    anywhere = pl.BlockSpec(memory_space=pl.ANY)
    return pl.pallas_call(
        functools.partial(butterfly_kernel, half, first_row),
        out_shape=jax.ShapeDtypeStruct((4, 8, BANDS, SLOT, 2 * HALF), jnp.bfloat16),
        in_specs=[anywhere, anywhere, anywhere, pl.BlockSpec(memory_space=pltpu.VMEM)] + [anywhere] * half,
        out_specs=anywhere,
        scratch_shapes=[
            pltpu.VMEM((BLOCKS, XROWS, PART), jnp.bfloat16),
            pltpu.VMEM((4, 12, PAIR, PAIR), jnp.bfloat16),
            pltpu.VMEM((4, 8, PAIR, PAIR), jnp.bfloat16),
            pltpu.VMEM((4, 8, BANDS, SLOT, HALF), jnp.bfloat16),
            pltpu.VMEM((16, PADR, PART), jnp.bfloat16),
            pltpu.VMEM((16, PADR, PART), jnp.bfloat16),
            pltpu.VMEM((BLOCKS, PADR, PART), jnp.bfloat16),
            pltpu.VMEM((4, 4, PADR, PART), jnp.bfloat16),
            pltpu.SemaphoreType.DMA((4,)),
            pltpu.SemaphoreType.DMA((4, 3)),
            pltpu.SemaphoreType.DMA((4,)),
            pltpu.SemaphoreType.DMA((4,)),
        ],
        input_output_aliases={4: 0} if half else {},
        compiler_params=pltpu.CompilerParams(vmem_limit_bytes=56 << 20),
        name="butterfly",
    )(rx, near, far, send_order(), *([rows] * half))


def mirror_order():
    row = lax.broadcasted_iota(jnp.int32, (256, 256), 0)
    lane = lax.broadcasted_iota(jnp.int32, (256, 256), 1)
    return (row + lane == 256).astype(jnp.bfloat16)


def fourier_kernel(u_ref, order_ref, mirror_ref, table_ref, middle_ref, out_ref, v, vt, edge, buf, sem):
    step = pl.program_id(0)
    slot = step % 2
    tile = 256

    def copies(at, into):
        near = pltpu.make_async_copy(buf.at[into, 0], out_ref.at[:, :, pl.ds((4 - at) * tile, tile)], sem.at[into, 0])
        far = pltpu.make_async_copy(buf.at[into, 1], out_ref.at[:, :, pl.ds((5 + at) * tile, tile)], sem.at[into, 1])
        return near, far

    def sums(table):
        even = jnp.dot(vt[:, :640], table[:640], preferred_element_type=jnp.float32)
        odd = jnp.dot(vt[:, 640:], table[640:], preferred_element_type=jnp.float32)
        return even, odd

    @pl.when(step == 0)
    def _():
        for g in range(16):
            piece = u_ref[pl.ds(8 * g, 8)].reshape(8 * SLOT, PART)
            y = jnp.dot(order_ref[...], piece, preferred_element_type=jnp.float32)
            for p in range(2):
                for r in range(5):
                    at = p * 200 + r * 40
                    v[r, pl.ds(p * 640 + 40 * g, 40), :] = y[at:at + 40].astype(jnp.bfloat16)
        for r in range(5):
            vt[pl.ds(r * PART, PART), :] = v[r].T
        even, odd = sums(middle_ref[...])
        edge[...] = even - odd

    @pl.when(step >= 2)
    def _():
        for copy in copies(step - 2, slot):
            copy.wait()

    even, odd = sums(table_ref[...])
    near = (even + odd).astype(jnp.bfloat16)
    far = (even - odd).astype(jnp.bfloat16)
    turned = jnp.dot(far, mirror_ref[...], preferred_element_type=jnp.float32)
    lane = lax.broadcasted_iota(jnp.int32, (5 * PART, 128), 1)
    head = jnp.where(lane == 0, edge[...], turned[:, :128]).astype(jnp.bfloat16)
    tail = turned[:, 128:].astype(jnp.bfloat16)
    edge[...] = far[:, :128].astype(jnp.float32)
    for r in range(5):
        rows = slice(r * PART, (r + 1) * PART)
        buf[slot, 0, r] = near[rows]
        buf[slot, 1, r, :, pl.ds(0, 128)] = head[rows]
        buf[slot, 1, r, :, pl.ds(128, 128)] = tail[rows]
    for copy in copies(step, slot):
        copy.start()

    @pl.when(step == 4)
    def _():
        for copy in copies(3, 1) + copies(4, 0):
            copy.wait()


def fourier(u, table):
    return pl.pallas_call(
        fourier_kernel,
        out_shape=jax.ShapeDtypeStruct((5, PART, NLON), jnp.bfloat16),
        grid=(5,),
        in_specs=[
            pl.BlockSpec((BLOCKS * BANDS, SLOT, PART), lambda j: (0, 0, 0)),
            pl.BlockSpec((400, 8 * SLOT), lambda j: (0, 0)),
            pl.BlockSpec((256, 256), lambda j: (0, 0)),
            pl.BlockSpec((1280, 256), lambda j: (0, 4 - j)),
            pl.BlockSpec((1280, 128), lambda j: (0, 10)),
        ],
        out_specs=pl.BlockSpec(memory_space=pl.ANY),
        scratch_shapes=[
            pltpu.VMEM((5, 1280, PART), jnp.bfloat16),
            pltpu.VMEM((5 * PART, 1280), jnp.bfloat16),
            pltpu.VMEM((5 * PART, 128), jnp.float32),
            pltpu.VMEM((2, 2, 5, PART, 256), jnp.bfloat16),
            pltpu.SemaphoreType.DMA((2, 2)),
        ],
        compiler_params=pltpu.CompilerParams(vmem_limit_bytes=60 << 20),
        name="fourier",
    )(u, receive_order(), mirror_order(), table, table)


def fourier_table(ids):
    longitude = jnp.arange(NLON // 2 + 128, dtype=jnp.int32)
    phases = ids[:, None] * longitude[None, :] % NLON
    angles = phases.astype(jnp.float32) * (2.0 * math.pi / NLON)
    weight = jnp.where(ids == 0, 1.0, 2.0).astype(jnp.float32) / math.sqrt(2.0 * ids.shape[0])
    cosine_part = weight[:, None] * jnp.cos(angles)
    sine_part = -weight[:, None] * jnp.sin(angles)
    return jnp.concatenate([cosine_part, sine_part], axis=0).astype(jnp.bfloat16)


def body(coefficients, factors, wave_ids):
    wave_pos = lax.axis_index("wave")
    lev_pos = lax.axis_index("lev")
    rx0 = lax.all_to_all(pack_first(factors, coefficients), "wave", 0, 0, tiled=True)
    send1, rx0 = lax.optimization_barrier((pack_second(coefficients), rx0))
    rx1 = lax.all_to_all(send1, "wave", 0, 0, tiled=True)
    own_ids = lax.dynamic_slice_in_dim(wave_ids, lev_pos * (OWN * BLOCKS) + wave_pos * OWN, OWN, 0)
    first = (own_ids[:, None] - jnp.arange(DEG, dtype=jnp.int32)[None, :]).reshape(ROWS)
    first = jnp.pad(first, (0, PADR - ROWS))
    first = jnp.broadcast_to(jnp.concatenate([first, first])[None, :], (8, PAIR))
    near, far = section_factors(rx0, first)
    rows = butterfly(rx0, FROWS, near, far, None)
    rows, rx1 = lax.optimization_barrier((rows, rx1))
    rows = butterfly(rx1, 0, near, far, rows).reshape(BLOCKS * BANDS, SLOT, 2 * HALF)
    u = lax.all_to_all(rows, ("wave", "lev"), 0, 0, tiled=True)
    ids = wave_ids.reshape(BANDS, BLOCKS, OWN).transpose(1, 0, 2).reshape(-1)
    return fourier(u, fourier_table(ids))


def solution(mesh):
    in_specs = (P("wave", "lev", None), P(None, None, "wave", None, "lev"), P())
    out_specs = P(("wave", "lev"), None, None)
    return jax.shard_map(body, mesh=mesh, in_specs=in_specs, out_specs=out_specs, check_vma=False)
```
